256 devices in a mesh: slab: 32 (over z_hi, x, y), chan: 8 (over z_lo, core).
Axes of the slice: x: 4, y: 4, z: 8 (z_hi: 2, z_lo: 4; z = z_hi * 4 + z_lo), core: 2. Of those that a mesh axis runs over, the one named last changes fastest.
Arguments:
- features: bfloat16 [96, 65536], P('chan', 'slab'), may hold values from -1 to 3
- coords: bfloat16 [3, 65536], P(None, 'slab'), may hold values from 0 to 1
- send_rows: int32 [2, 32768], P(None, 'slab'), may hold values from 0 to 2047
- send_count: int32 [2, 32], P(None, 'slab'), may hold values from 1 to 1024, as said below
- neighbours: int32 [4096, 128], P('slab'), may hold values from 0 to 4095, as said below
- neighbour_count: int32 [4096], P('slab'), may hold values from 32 to 128
- geom_weight: bfloat16 [80, 6], replicated, may hold values from -3.5 to 3.5
- feat_weight: bfloat16 [80, 96], replicated, may hold values from -0.625 to 0.625
- bias_one: float32 [80], replicated, may hold values from -3 to 3
- hidden_weight: bfloat16 [80, 80], replicated, may hold values from -1 to 1
- bias_two: float32 [80], replicated, may hold values from -3 to 3
- out_weight: bfloat16 [96, 80], replicated, may hold values from -1 to 1
- bias_three: float32 [96], replicated, may hold values from -3 to 3
Outputs:
- latent: float32 [96, 4096], P('chan', 'slab')
The draws below stay inside these ranges and needn't reach their ends.
Inputs may be any that keep to these rules, and one draw needn't show every extreme that they name: `send_count`: every slab has at least one live slot in each direction; some slab has all 1024 slots of its lower list live. `neighbours`: entries index the slab's point table: below 2048 own points, then 1024 slots from the slab below, then 1024 from the slab above; slot 0 of every node is an own point; nodes of the lower plane of a slab use the slots from below, those of the upper plane the slots from above, and may name dead slots.
All inputs are finite; a program needn't handle non-finite values.
Results may differ from the reference program's by a relative error of at most 0.0013.
Values may be sent and summed in bfloat16 or wider, within the bound.
A program may use at most 64 MiB of HBM per device.

```python
import jax
import jax.numpy as jnp
from jax import lax

F = 96
KH = 80
K = 128
ZD = 2
GX = 16
GY = 4
PTS_DEV = 2048
SEND = 1024
POINTS = 65536
NODES = 4096
N_SLAB = 32


def draw_send_count(key, part):
    counts = jax.random.randint(jax.random.fold_in(key, 7), (2, N_SLAB), 1, SEND + 1)
    return counts.at[0, 0].set(SEND).astype(jnp.int32)


def draw_neighbours(key, part):
    keys = jax.random.split(jax.random.fold_in(key, 11), 3)
    local = jax.random.randint(keys[0], (NODES, K), 0, PTS_DEV)
    slot = jax.random.randint(keys[1], (NODES, K), 0, SEND)
    kind = jax.random.randint(keys[2], (NODES, K), 0, 10)
    plane = jnp.arange(NODES, dtype=jnp.int32) // (GX * GY) % ZD
    side = jnp.where(plane < ZD // 2, PTS_DEV, PTS_DEV + SEND)
    picked = jnp.where(kind < 4, side[:, None] + slot, local)
    picked = picked.at[:, 0].set(local[:, 0])
    return picked.astype(jnp.int32)


def set_ends(values, rng, low, top_value):
    longest = values.shape.index(max(values.shape))
    spots = []
    for shift in (0, 1):
        where = [jax.random.randint(jax.random.fold_in(rng, axis), (), 0, length) for axis, length in enumerate(values.shape)]
        where[longest] = (where[longest] + shift) % values.shape[longest]
        spots.append(tuple(where))
    return values.at[spots[0]].set(low).at[spots[1]].set(top_value)


def steps_of(rng, extent, pieces, smallest, high):
    level, own = 1.0, jax.random.fold_in(rng, 6)
    for position, blocks in pieces:
        draws = jnp.exp(jax.random.uniform(jax.random.fold_in(own, position), (blocks,), jnp.float32, smallest / len(pieces), high / len(pieces)))
        level = level * jnp.repeat(draws, extent[position] // blocks).reshape([-1 if axis == position else 1 for axis in range(len(extent))])
    return level


def scatter_about(own_key, extent, scale, most, held_as=jnp.bfloat16):
    entries = jax.random.normal(own_key, extent, jnp.float32) * scale
    return jnp.minimum(jnp.maximum(entries, -most), most).astype(held_as)


def setup_inputs(seed: int = 0) -> dict:
    seeds = jax.random.split(jax.random.key(seed), 14)
    return {
        "features": jnp.clip(-1.0 + 4.0 * jax.random.uniform(seeds[0], (F, POINTS), jnp.float32) ** steps_of(seeds[0], (F, POINTS), ((0, 8), (1, 32)), -0.2, 0.2), -1.0, 3.0).astype(jnp.bfloat16),
        "coords": jnp.clip(1.0 * jax.random.uniform(seeds[1], (3, POINTS), jnp.float32) ** steps_of(seeds[1], (3, POINTS), ((1, 32),), -0.2, 0.2), 0.0, 1.0).astype(jnp.bfloat16),
        "send_rows": set_ends(jax.random.randint(seeds[2], (2, SEND * N_SLAB), 0, PTS_DEV), jax.random.fold_in(seeds[2], 1), 0, PTS_DEV - 1).astype(jnp.int32),
        "send_count": draw_send_count(jax.random.fold_in(seeds[13], 71), 0),
        "neighbours": draw_neighbours(jax.random.fold_in(seeds[13], 71), 0),
        "neighbour_count": set_ends(jax.random.randint(seeds[5], (NODES,), K // 4, K + 1), jax.random.fold_in(seeds[5], 1), K // 4, K).astype(jnp.int32),
        "geom_weight": scatter_about(seeds[6], (KH, 6), 3 ** -0.5, 3.5),
        "feat_weight": scatter_about(seeds[7], (KH, F), F ** -0.5, 0.625),
        "bias_one": scatter_about(seeds[8], (KH,), 0.5, 3.0, jnp.float32),
        "hidden_weight": scatter_about(seeds[9], (KH, KH), (KH // 2) ** -0.5, 1.0),
        "bias_two": scatter_about(seeds[10], (KH,), 0.5, 3.0, jnp.float32),
        "out_weight": scatter_about(seeds[11], (F, KH), (KH // 2) ** -0.5, 1.0),
        "bias_three": scatter_about(seeds[12], (F,), 0.5, 3.0, jnp.float32),
    }


def node_term(geom_weight, bias_one, node_ids, depth):
    along_x = ((node_ids % GX).astype(jnp.float32) + 0.5) / GX
    along_y = (((node_ids // GX) % GY).astype(jnp.float32) + 0.5) / GY
    along_z = ((node_ids // (GX * GY)).astype(jnp.float32) + 0.5) / depth
    geom = geom_weight[:, 0:3].astype(jnp.float32)
    return (geom[:, 0:1] * along_x[None, :] + geom[:, 1:2] * along_y[None, :]
            + geom[:, 2:3] * along_z[None, :] + bias_one[:, None])


def kernel_block(pre_table, value_table, flag_table, nbr, counts, node_pre, hidden_weight, bias_two, out_rows, bias_rows):
    nodes, slots = nbr.shape
    hidden = pre_table.shape[0]
    flat = nbr.reshape(-1)
    gathered = jnp.take(pre_table, flat, axis=1).astype(jnp.float32).reshape(hidden, nodes, slots)
    first = jax.nn.gelu(gathered + node_pre[:, :, None]).reshape(hidden, nodes * slots).astype(jnp.bfloat16)
    second = jax.nn.gelu(jnp.dot(hidden_weight, first, preferred_element_type=jnp.float32) + bias_two[:, None]).astype(jnp.bfloat16)
    kappa = jnp.dot(out_rows, second, preferred_element_type=jnp.float32) + bias_rows[:, None]
    values = jnp.take(value_table, flat, axis=1).astype(jnp.float32)
    used = (jnp.arange(slots, dtype=jnp.int32)[None, :] < counts[:, None]).astype(jnp.float32)
    flags = jnp.take(flag_table, flat).astype(jnp.float32) * used.reshape(-1)
    total = (kappa * values * flags[None, :]).reshape(out_rows.shape[0], nodes, slots).sum(axis=2)
    weight = flags.reshape(nodes, slots).sum(axis=1)
    return total / weight[None, :]


def encode(pre_table, value_table, flag_table, nbr, counts, first_id, depth, geom_weight, bias_one, hidden_weight, bias_two, out_rows, bias_rows):
    nodes = nbr.shape[0]
    block = min(128, nodes)
    blocks = nodes // block

    def one_block(index):
        start = index * block
        ids = first_id + start + jnp.arange(block, dtype=jnp.int32)
        node_pre = node_term(geom_weight, bias_one, ids, depth)
        part_nbr = lax.dynamic_slice_in_dim(nbr, start, block, 0)
        part_cnt = lax.dynamic_slice_in_dim(counts, start, block, 0)
        return kernel_block(pre_table, value_table, flag_table, part_nbr, part_cnt, node_pre, hidden_weight, bias_two, out_rows, bias_rows)

    result = lax.map(one_block, jnp.arange(blocks, dtype=jnp.int32))
    return result.transpose(1, 0, 2).reshape(out_rows.shape[0], nodes)


def reference(features, coords, send_rows, send_count, neighbours, neighbour_count, geom_weight, feat_weight, bias_one, hidden_weight, bias_two, out_weight, bias_three):
    slabs = N_SLAB
    pts = PTS_DEV
    send = SEND
    pre = (jnp.dot(feat_weight, features, preferred_element_type=jnp.float32)
           + jnp.dot(geom_weight[:, 3:6], coords, preferred_element_type=jnp.float32)).astype(jnp.bfloat16)
    offsets = (jnp.arange(slabs, dtype=jnp.int32) * pts)[None, :, None]
    rows = (send_rows.reshape(2, slabs, send) + offsets).reshape(-1)
    live = (jnp.arange(send, dtype=jnp.int32)[None, None, :] < send_count[:, :, None]).astype(jnp.bfloat16)
    pre_send = jnp.take(pre, rows, axis=1).reshape(KH, 2, slabs, send) * live[None]
    feat_send = jnp.take(features, rows, axis=1).reshape(F, 2, slabs, send) * live[None]

    def from_below(x):
        return jnp.concatenate([jnp.zeros_like(x[..., :1, :]), x[..., :-1, :]], axis=-2)

    def from_above(x):
        return jnp.concatenate([x[..., 1:, :], jnp.zeros_like(x[..., :1, :])], axis=-2)

    pre_tables = jnp.concatenate([pre.reshape(KH, slabs, pts), from_below(pre_send[:, 1]), from_above(pre_send[:, 0])], axis=2)
    value_tables = jnp.concatenate([features.reshape(F, slabs, pts), from_below(feat_send[:, 1]), from_above(feat_send[:, 0])], axis=2)
    flag_tables = jnp.concatenate([jnp.ones((slabs, pts), jnp.bfloat16), from_below(live[1]), from_above(live[0])], axis=1)
    per_slab = ZD * GY * GX
    nbr = neighbours.reshape(slabs, per_slab, K)
    cnt = neighbour_count.reshape(slabs, per_slab)
    depth = ZD * slabs

    def one_slab(index):
        return encode(pre_tables[:, index], value_tables[:, index], flag_tables[index], nbr[index], cnt[index],
                      index * per_slab, depth, geom_weight, bias_one, hidden_weight, bias_two, out_weight, bias_three)

    outs = lax.map(one_slab, jnp.arange(slabs, dtype=jnp.int32))
    return outs.transpose(1, 0, 2).reshape(F, slabs * per_slab)
```

```python
import functools

import jax
import jax.numpy as jnp
from jax import lax
from jax.experimental import pallas as pl
from jax.experimental.pallas import tpu as pltpu
from jax.sharding import PartitionSpec as P

MESH = pl.DeviceIdType.MESH
ZD = 2
GX = 16
GY = 4
F32 = jnp.float32
BF16 = jnp.bfloat16
ROWS = 16
BLK = 256
C0 = 0.7978845608028654
C1 = 0.7978845608028654 * 0.044715


def gelu(x):
    half = 0.5 * x
    return half + half * jnp.tanh(x * (C0 + C1 * (x * x)))


def iota(shape, dim):
    return lax.broadcasted_iota(jnp.int32, shape, dim)


def one_hot(index, ramp):
    row = jnp.broadcast_to(index, (16, index.shape[1])).astype(BF16)
    full = jnp.concatenate([row] * (BLK // 16), axis=0)
    return jnp.where(ramp == full, jnp.ones_like(full), jnp.zeros_like(full))


def kernel(
    slabs,
    feat,
    coords,
    send_rows,
    send_count,
    nbr,
    counts,
    geom_t,
    feat_weight,
    bias_one,
    hidden_weight,
    bias_two,
    out_t,
    bias_three,
    out,
    own,
    halo,
    picked,
    hot,
    grid,
    stage,
    small,
    wide,
    w_pre,
    w_out,
    res,
    rcv,
    own_send,
    own_recv,
    own_fwd,
    halo_send,
    halo_recv,
    halo_fwd,
    res_send,
    res_recv,
):
    s = lax.axis_index("slab")
    c = lax.axis_index("chan")
    chip = c // 2
    core = c % 2
    sib = c + 1 - 2 * core
    upper = c // 4
    has_up = s < slabs - 1
    has_down = s > 0
    has_halo = jnp.where(upper == 1, s < slabs - 1, s > 0)
    source_slab = s - 1 + 2 * upper
    points = feat.shape[1]
    send = send_rows.shape[1]

    barrier = pltpu.get_barrier_semaphore()
    for j in range(1, 8):
        pl.semaphore_signal(barrier, inc=1, device_id=(s, (c + j) % 8), device_id_type=MESH)

    @pl.when(has_halo)
    def _():
        for q in range(4):
            pl.semaphore_signal(
                barrier, inc=1, device_id=(source_slab, 2 * q + core), device_id_type=MESH
            )

    stage[0:12, :] = feat[...].astype(F32)
    stage[12:15, :] = coords[...].astype(F32)
    stage[15:16, :] = jnp.ones((1, points), F32)
    slot = stage[...].astype(BF16)
    own[c] = slot

    ramp = iota((BLK, 128), 0).astype(F32).astype(BF16)
    pieces = points // BLK
    stacked = jnp.concatenate([slot[:, h * BLK : (h + 1) * BLK] for h in range(pieces)], axis=0)
    for d in range(2):
        for j in range(send // BLK):
            idx = send_rows[d : d + 1, j * BLK : (j + 1) * BLK]
            idx = jnp.where(iota((1, BLK), 1) + j * BLK < send_count[d], idx, -1)
            low = (idx & (BLK - 1)).astype(F32)
            high = lax.shift_right_arithmetic(idx, 8)
            hots = jnp.concatenate(
                [one_hot(low[:, t * 128 : (t + 1) * 128], ramp) for t in range(BLK // 128)], axis=1
            )
            parts = jnp.dot(stacked, hots, preferred_element_type=F32)
            total = jnp.zeros((ROWS, BLK), F32)
            for h in range(pieces):
                total = total + jnp.where(high == h, parts[h * ROWS : (h + 1) * ROWS], 0.0)
            picked[d, :, j * BLK : (j + 1) * BLK] = total.astype(BF16)

    pl.semaphore_wait(barrier, 7 + 2 * jnp.where(has_up, 1, 0) + 2 * jnp.where(has_down, 1, 0))

    def halo_copy(d, q):
        target = (s + 1, 2 * q + core) if d == 1 else (s - 1, 4 + 2 * q + core)
        return pltpu.make_async_remote_copy(
            src_ref=picked.at[d],
            dst_ref=halo.at[c],
            send_sem=halo_send.at[d, q],
            recv_sem=halo_recv.at[c],
            device_id=target,
            device_id_type=MESH,
        )

    def own_copy(j):
        target = sib if j == 0 else 2 * ((chip + j) % 4) + core
        return pltpu.make_async_remote_copy(
            src_ref=own.at[c],
            dst_ref=own.at[c],
            send_sem=own_send.at[j],
            recv_sem=own_recv.at[c],
            device_id=(s, target),
            device_id_type=MESH,
        )

    @pl.when(has_up)
    def _():
        for q in range(2):
            halo_copy(1, q).start()

    @pl.when(has_down)
    def _():
        for q in range(2):
            halo_copy(0, q).start()

    for j in range(4):
        own_copy(j).start()

    small[...] = jnp.zeros_like(small)
    small[0:6, 0:80] = geom_t[...].astype(F32)
    small[6:7, 0:80] = bias_one[...]
    small[7:8, 0:80] = bias_two[...]
    lane = iota((96, 128), 1)
    spread = jnp.where(
        (lane // ROWS * 12 + lane % ROWS == iota((96, 128), 0)) & (lane % ROWS < 12), 1.0, 0.0
    )
    b3 = jnp.dot(
        jnp.broadcast_to(bias_three[...], (8, 96)),
        spread,
        preferred_element_type=F32,
        precision=lax.Precision.HIGHEST,
    )
    small[8:16, :] = jnp.where(iota((8, 128), 1) % ROWS == ROWS - 1, 1.0, b3)
    cols = jnp.transpose(small[...])
    spread = spread.astype(BF16)
    lane80 = iota((80, 128), 1)
    wide_pre = jnp.dot(feat_weight[...], spread, preferred_element_type=F32)
    for i in range(3):
        wide_pre = jnp.where(lane80 == 12 + i, cols[0:80, 3 + i : 4 + i], wide_pre)
    w_pre[...] = wide_pre.astype(BF16)
    small[0:80, :] = jnp.dot(out_t[...], spread, preferred_element_type=F32)
    w_out[...] = jnp.transpose(small[...])[:, 0:80].astype(BF16)
    along_y = ((c % GY).astype(F32) + 0.5) / GY
    along_z = ((2 * s + upper).astype(F32) + 0.5) / (ZD * slabs)
    wide[0:80, :] = jnp.broadcast_to(cols[0:80, 0:1], (80, 128))
    wide[80:160, :] = jnp.broadcast_to(
        cols[0:80, 1:2] * along_y + cols[0:80, 2:3] * along_z + cols[0:80, 6:7], (80, 128)
    )
    wide[160:240, :] = jnp.broadcast_to(cols[0:80, 7:8], (80, 128))
    wide[240:368, :] = jnp.broadcast_to(cols[:, 8:9], (128, 128))

    first = pl.multiple_of(c * 16, 16)
    idx = nbr[pl.ds(first, 16), :]
    idx = idx - jnp.where(idx >= points, send * upper, 0)
    slots = iota((1, 128), 1)
    rows = []
    for n in range(16):
        rows.append(jnp.where(slots < counts[first + n], idx[n : n + 1, :], -1))
    lows = [(r & (BLK - 1)).astype(F32) for r in rows]
    highs = [lax.shift_right_arithmetic(r, 8) for r in rows]

    def build(kb, carry):
        at = pl.ds(pl.multiple_of(kb * BLK, BLK), BLK)
        for n in range(16):
            pick = jnp.where(highs[n] == kb, lows[n], -1.0)
            hot[at, n * 128 : (n + 1) * 128] = one_hot(pick, ramp)
        return carry

    lax.fori_loop(0, (points + send) // BLK, build, 0)

    def landed(buf, sem, i):
        return pltpu.make_async_remote_copy(
            src_ref=buf.at[i],
            dst_ref=buf.at[i],
            send_sem=sem.at[i],
            recv_sem=sem.at[i],
            device_id=(s, sib),
            device_id_type=MESH,
        )

    def forward(buf, fwd, recv, i, k):
        return pltpu.make_async_remote_copy(
            src_ref=buf.at[i],
            dst_ref=buf.at[i],
            send_sem=fwd.at[k],
            recv_sem=recv.at[i],
            device_id=(s, sib),
            device_id_type=MESH,
        )

    for j in range(1, 4):
        i = 2 * ((chip + j) % 4) + core
        landed(own, own_recv, i).wait_recv()
        forward(own, own_fwd, own_recv, i, j - 1).start()
    for j in range(4):
        landed(own, own_recv, 2 * ((chip + j) % 4) + 1 - core).wait_recv()

    table = own[...].reshape(8 * ROWS, points)

    def gather_own(b, carry):
        at = pl.ds(pl.multiple_of(b * BLK, BLK), BLK)
        grid[:, at] = jnp.dot(table, hot[0:points, at], preferred_element_type=F32)
        return carry

    lax.fori_loop(0, 2048 // BLK, gather_own, 0)

    @pl.when(has_halo)
    def _():
        for q in range(4):
            i = 2 * q + core
            landed(halo, halo_recv, i).wait_recv()
            forward(halo, halo_fwd, halo_recv, i, q).start()
        for q in range(4):
            landed(halo, halo_recv, 2 * q + 1 - core).wait_recv()

    @pl.when(jnp.logical_not(has_halo))
    def _():
        halo[...] = jnp.zeros_like(halo)

    side = halo[...].reshape(8 * ROWS, send)
    w1 = w_pre[...]
    w2 = hidden_weight[...]
    w3 = w_out[...]

    def block(b, acc):
        at = pl.ds(pl.multiple_of(b * BLK, BLK), BLK)
        values = grid[:, at] + jnp.dot(
            side, hot[points : points + send, at], preferred_element_type=F32
        )
        pre = jnp.dot(w1, values.astype(BF16), preferred_element_type=F32)
        pre = pre.astype(BF16).astype(F32)
        x0 = ((2 * b).astype(F32) + 0.5) / GX
        x1 = ((2 * b + 1).astype(F32) + 0.5) / GX
        base = wide[80:160, :]
        slope = wide[0:80, :]
        node = jnp.concatenate([base + slope * x0, base + slope * x1], axis=1)
        h1 = gelu(pre + node).astype(BF16)
        b2 = wide[160:240, :]
        h2 = jnp.dot(w2, h1, preferred_element_type=F32) + jnp.concatenate([b2, b2], axis=1)
        h2 = gelu(h2).astype(BF16)
        b3w = wide[240:368, :]
        kappa = jnp.dot(w3, h2, preferred_element_type=F32) + jnp.concatenate([b3w, b3w], axis=1)
        prod = kappa * values
        top = prod.astype(BF16)
        rest = (prod - top.astype(F32)).astype(BF16)
        place = c * 16 + 2 * b + iota((BLK, 128), 0) // 128
        seg = jnp.where(iota((BLK, 128), 1) == place, 1.0, 0.0).astype(BF16)
        return (
            acc
            + jnp.dot(top, seg, preferred_element_type=F32)
            + jnp.dot(rest, seg, preferred_element_type=F32)
        )

    acc = lax.fori_loop(0, 2048 // BLK, block, jnp.zeros((128, 128), F32))
    mine = iota((128, 128), 1) // 16 == c
    number = jnp.where(mine, jnp.broadcast_to(acc[15:16, :], (128, 128)), 1.0)
    res[...] = jnp.where(mine, acc / number, 0.0).reshape(8, ROWS, 128)

    def res_copy(j):
        target = (c + j) % 8
        return pltpu.make_async_remote_copy(
            src_ref=res.at[target],
            dst_ref=rcv.at[c],
            send_sem=res_send.at[j - 1],
            recv_sem=res_recv.at[c],
            device_id=(s, target),
            device_id_type=MESH,
        )

    for j in range(1, 8):
        res_copy(j).start()
    rcv[c] = res[c]

    for j in range(4):
        own_copy(j).wait_send()
    for j in range(1, 4):
        i = 2 * ((chip + j) % 4) + core
        forward(own, own_fwd, own_recv, i, j - 1).wait_send()

    @pl.when(has_up)
    def _():
        for q in range(2):
            halo_copy(1, q).wait_send()

    @pl.when(has_down)
    def _():
        for q in range(2):
            halo_copy(0, q).wait_send()

    @pl.when(has_halo)
    def _():
        for q in range(4):
            forward(halo, halo_fwd, halo_recv, 2 * q + core, q).wait_send()

    for j in range(1, 8):
        landed(rcv, res_recv, (c + j) % 8).wait_recv()
    for j in range(1, 8):
        res_copy(j).wait_send()
    out[...] = rcv[...].sum(axis=0)[0:12, :]


def shards(
    slabs,
    features,
    coords,
    send_rows,
    send_count,
    neighbours,
    neighbour_count,
    geom_weight,
    feat_weight,
    bias_one,
    hidden_weight,
    bias_two,
    out_weight,
    bias_three,
):
    points = features.shape[1]
    send = send_rows.shape[1]
    vmem = pl.BlockSpec(memory_space=pltpu.VMEM)
    smem = pl.BlockSpec(memory_space=pltpu.SMEM)
    dma = pltpu.SemaphoreType.DMA
    return pl.pallas_call(
        functools.partial(kernel, slabs),
        out_shape=jax.ShapeDtypeStruct((12, 128), F32),
        in_specs=[vmem, vmem, vmem, smem, vmem, smem] + [vmem] * 7,
        out_specs=vmem,
        scratch_shapes=[
            pltpu.VMEM((8, ROWS, points), BF16),
            pltpu.VMEM((8, ROWS, send), BF16),
            pltpu.VMEM((2, ROWS, send), BF16),
            pltpu.VMEM((points + send, 2048), BF16),
            pltpu.VMEM((8 * ROWS, 2048), F32),
            pltpu.VMEM((ROWS, points), F32),
            pltpu.VMEM((128, 128), F32),
            pltpu.VMEM((368, 128), F32),
            pltpu.VMEM((80, 128), BF16),
            pltpu.VMEM((128, 80), BF16),
            pltpu.VMEM((8, ROWS, 128), F32),
            pltpu.VMEM((8, ROWS, 128), F32),
            dma((4,)),
            dma((8,)),
            dma((3,)),
            dma((2, 2)),
            dma((8,)),
            dma((4,)),
            dma((7,)),
            dma((8,)),
        ],
        compiler_params=pltpu.CompilerParams(
            collective_id=0, has_side_effects=True, vmem_limit_bytes=60 * 2**20
        ),
    )(
        features,
        coords,
        send_rows,
        send_count.reshape(2),
        neighbours,
        neighbour_count,
        geom_weight.T,
        feat_weight,
        bias_one.reshape(1, -1),
        hidden_weight,
        bias_two.reshape(1, -1),
        out_weight.T,
        bias_three.reshape(1, -1),
    )


def solution(mesh):
    placed = (
        P("chan", "slab"),
        P(None, "slab"),
        P(None, "slab"),
        P(None, "slab"),
        P("slab", None),
        P("slab"),
        P(),
        P(),
        P(),
        P(),
        P(),
        P(),
        P(),
    )
    return jax.shard_map(
        functools.partial(shards, mesh.shape["slab"]),
        mesh=mesh,
        in_specs=placed,
        out_specs=P("chan", "slab"),
        check_vma=False,
    )
```

```python
import functools

import jax
import jax.numpy as jnp
from jax import lax
from jax.experimental import pallas as pl
from jax.experimental.pallas import tpu as pltpu
from jax.sharding import PartitionSpec as P

MESH = pl.DeviceIdType.MESH
ZD = 2
GX = 16
GY = 4
F32 = jnp.float32
BF16 = jnp.bfloat16
ROWS = 16
BLK = 256
C0 = 0.7978845608028654
C1 = 0.7978845608028654 * 0.044715


def gelu(x):
    half = 0.5 * x
    return half + half * jnp.tanh(x * (C0 + C1 * (x * x)))


def iota(shape, dim):
    return lax.broadcasted_iota(jnp.int32, shape, dim)


def one_hot(index, ramp):
    row = jnp.broadcast_to(index, (16, index.shape[1])).astype(BF16)
    full = jnp.concatenate([row] * (BLK // 16), axis=0)
    return jnp.where(ramp == full, jnp.ones_like(full), jnp.zeros_like(full))


def kernel(
    slabs,
    feat_h,
    coords_h,
    send_rows_h,
    send_count_h,
    nbr_h,
    counts_h,
    geom_h,
    feat_weight_h,
    bias_one_h,
    hidden_weight_h,
    bias_two_h,
    out_weight_h,
    bias_three_h,
    out,
    feat,
    coords,
    send_rows,
    send_count,
    nbr,
    counts,
    geom_t,
    feat_weight,
    bias_one,
    hidden_weight,
    bias_two,
    out_t,
    bias_three,
    own,
    halo,
    picked,
    side_out,
    side_in,
    table,
    hot,
    grid,
    node,
    stage,
    pack,
    small,
    wide,
    w_pre,
    w_out,
    res,
    rcv,
    in_sem,
    own_send,
    own_recv,
    own_fwd,
    relay_send,
    halo_send,
    halo_recv,
    halo_fwd,
    side_send,
    side_recv,
    res_send,
    res_recv,
):
    s = lax.axis_index("slab")
    c = lax.axis_index("chan")
    chip = c // 2
    core = c % 2
    sib = c + 1 - 2 * core
    upper = c // 4
    inner = (chip == 1) | (chip == 2)
    has_up = s < slabs - 1
    has_down = s > 0
    has_halo = jnp.where(upper == 1, s < slabs - 1, s > 0)
    source_slab = s - 1 + 2 * upper
    points = feat.shape[1]
    send = send_rows.shape[1]
    body = points * 3 // 4
    tail = points - body
    hbody = send * 3 // 4
    htail = send - hbody
    pairs = node.shape[1]

    barrier = pltpu.get_barrier_semaphore()
    for j in range(1, 8):
        pl.semaphore_signal(barrier, inc=1, device_id=(s, (c + j) % 8), device_id_type=MESH)

    @pl.when(has_halo)
    def _():
        for q in range(4):
            pl.semaphore_signal(
                barrier, inc=1, device_id=(source_slab, 2 * q + core), device_id_type=MESH
            )

    loads = [
        pltpu.make_async_copy(a, b, in_sem.at[i])
        for i, (a, b) in enumerate(
            [
                (feat_h, feat),
                (coords_h, coords),
                (send_rows_h, send_rows),
                (send_count_h, send_count),
                (nbr_h, nbr),
                (counts_h, counts),
                (geom_h, geom_t),
                (feat_weight_h, feat_weight),
                (bias_one_h, bias_one),
                (hidden_weight_h, hidden_weight),
                (bias_two_h, bias_two),
                (out_weight_h, out_t),
                (bias_three_h, bias_three),
            ]
        )
    ]
    for load in loads:
        load.start()
    for load in loads[:4]:
        load.wait()

    values = feat[...].astype(F32)
    pack[0:12, :] = values[:, 0:body]
    for g in range(3):
        pack[12:16, g * tail : (g + 1) * tail] = values[4 * g : 4 * g + 4, body:points]
    own[c] = pack[...].astype(BF16)

    stage[0:12, :] = values
    stage[12:15, :] = coords[...].astype(F32)
    stage[15:16, :] = jnp.ones((1, points), F32)
    slot = stage[...].astype(BF16)

    ramp = iota((BLK, 128), 0).astype(F32).astype(BF16)
    pieces = points // BLK
    stacked = jnp.concatenate([slot[:, h * BLK : (h + 1) * BLK] for h in range(pieces)], axis=0)
    lists = []
    for d in range(2):
        idx = send_rows[d : d + 1, :]
        idx = jnp.where(iota((1, send), 1) < send_count[d], idx, -1)
        low = (idx & (BLK - 1)).astype(F32)
        high = lax.shift_right_arithmetic(idx, 8)
        hots = jnp.concatenate(
            [one_hot(low[:, t * 128 : (t + 1) * 128], ramp) for t in range(send // 128)], axis=1
        )
        parts = jnp.dot(stacked, hots, preferred_element_type=F32)
        total = jnp.zeros((ROWS, send), F32)
        for h in range(pieces):
            total = total + jnp.where(high == h, parts[h * ROWS : (h + 1) * ROWS], 0.0)
        pack[0:12, 0:hbody] = total[0:12, 0:hbody]
        for g in range(3):
            pack[12:16, g * htail : (g + 1) * htail] = total[4 * g : 4 * g + 4, hbody:send]
        picked[d] = pack[:, 0:hbody].astype(BF16)
        lists.append(total[12:16, :])
    mine = jnp.where(upper == 1, lists[0], lists[1])
    for j in range(4):
        pack[4 * j : 4 * j + 4, 0:htail] = mine[:, j * htail : (j + 1) * htail]
    side_out[...] = pack[:, 0:htail].astype(BF16)

    pl.semaphore_wait(barrier, 7 + 2 * jnp.where(has_up, 1, 0) + 2 * jnp.where(has_down, 1, 0))

    def remote(src, dst, sem_out, sem_in, target):
        return pltpu.make_async_remote_copy(
            src_ref=src,
            dst_ref=dst,
            send_sem=sem_out,
            recv_sem=sem_in,
            device_id=target,
            device_id_type=MESH,
        )

    def halo_copy(d, q):
        target = (s + 1, 2 * q + core) if d == 1 else (s - 1, 4 + 2 * q + core)
        return remote(picked.at[d], halo.at[c], halo_send.at[d, q], halo_recv.at[c], target)

    def side_copy():
        return remote(
            side_out, side_in, side_send.at[0], side_recv.at[0], (s + 1 - 2 * upper, c)
        )

    def own_copy(j):
        target = sib if j == 0 else 2 * ((chip + j) % 4) + core
        return remote(own.at[c], own.at[c], own_send.at[j], own_recv.at[c], (s, target))

    def own_far(j):
        there = (chip + j) % 4
        return (jnp.abs(there - chip) == 2) & inner

    def when_own(j, act):
        if j == 0:
            act(own_copy(0))
        else:

            @pl.when(jnp.logical_not(own_far(j)))
            def _():
                act(own_copy(j))

    sends_side = jnp.where(upper == 1, s > 0, s < slabs - 1)

    @pl.when(has_up)
    def _():
        for q in range(2):
            halo_copy(1, q).start()

    @pl.when(has_down)
    def _():
        for q in range(2):
            halo_copy(0, q).start()

    @pl.when(sends_side)
    def _():
        side_copy().start()

    for j in range(4):
        when_own(j, lambda copy: copy.start())

    for load in loads[4:]:
        load.wait()
    small[...] = jnp.zeros_like(small)
    small[0:6, 0:80] = geom_t[...].astype(F32)
    small[6:7, 0:80] = bias_one[...]
    small[7:8, 0:80] = bias_two[...]
    lane = iota((96, 128), 1)
    spread = jnp.where(
        (lane // ROWS * 12 + lane % ROWS == iota((96, 128), 0)) & (lane % ROWS < 12), 1.0, 0.0
    )
    small[8:16, :] = jnp.dot(
        jnp.broadcast_to(bias_three[...], (8, 96)),
        spread,
        preferred_element_type=F32,
        precision=lax.Precision.HIGHEST,
    )
    cols = jnp.transpose(small[...])
    spread = spread.astype(BF16)
    w_pre[:, 0:128] = jnp.dot(feat_weight[...], spread, preferred_element_type=F32).astype(BF16)
    lane16 = iota((80, 16), 1)
    w_side = jnp.zeros((80, 16), F32)
    for i in range(3):
        w_side = jnp.where(lane16 == i, cols[0:80, 3 + i : 4 + i], w_side)
    w_pre[:, 128:144] = w_side.astype(BF16)
    small[0:80, :] = jnp.dot(out_t[...], spread, preferred_element_type=F32)
    w_out[...] = jnp.transpose(small[...])[:, 0:80].astype(BF16)
    along_y = ((c % GY).astype(F32) + 0.5) / GY
    along_z = ((2 * s + upper).astype(F32) + 0.5) / (ZD * slabs)
    wide[0:80, :] = jnp.broadcast_to(cols[0:80, 7:8], (80, 128))
    wide[80:208, :] = jnp.broadcast_to(cols[:, 8:9], (128, 128))
    slope = jnp.broadcast_to(cols[0:80, 0:1], (80, 128))
    base = jnp.broadcast_to(
        cols[0:80, 1:2] * along_y + cols[0:80, 2:3] * along_z + cols[0:80, 6:7], (80, 128)
    )
    for n in range(16):
        node[:, n * 128 : (n + 1) * 128] = base + slope * ((n + 0.5) / GX)

    first = pl.multiple_of(c * 16, 16)
    idx = nbr[pl.ds(first, 16), :]
    idx = idx - jnp.where(idx >= points, send * upper, 0)
    slots = iota((1, 128), 1)
    rows = []
    for n in range(16):
        rows.append(jnp.where(slots < counts[first + n], idx[n : n + 1, :], -1))
    lows = [(r & (BLK - 1)).astype(F32) for r in rows]
    highs = [lax.shift_right_arithmetic(r, 8) for r in rows]

    def build(kb, carry):
        at = pl.ds(pl.multiple_of(kb * BLK, BLK), BLK)
        for n in range(16):
            pick = jnp.where(highs[n] == kb, lows[n], -1.0)
            hot[at, n * 128 : (n + 1) * 128] = one_hot(pick, ramp)
        return carry

    lax.fori_loop(0, (points + send) // BLK, build, 0)
    extra = jnp.concatenate(
        [coords[...].astype(F32), jnp.ones((1, points), F32), jnp.zeros((12, points), F32)], axis=0
    )
    table[128:144, 0:points] = extra.astype(BF16)

    def landed(buf, sem, i):
        return remote(buf.at[i], buf.at[i], sem.at[i], sem.at[i], (s, sib))

    def forward(buf, fwd, recv, i, k):
        return remote(buf.at[i], buf.at[i], fwd.at[k], recv.at[i], (s, sib))

    def relay():
        i = 2 * (3 - chip) + core
        return remote(
            own.at[i], own.at[i], relay_send.at[0], own_recv.at[i], (s, 6 * (chip - 1) + core)
        )

    for j in range(1, 4):
        there = jnp.where(inner, (3 - chip + j - 1) % 4, (chip + j) % 4)
        there = jnp.where(inner & (j > 1), jnp.where(j == 2, 0, 3), there)
        i = 2 * there + core
        landed(own, own_recv, i).wait_recv()
        if j == 1:

            @pl.when(inner)
            def _():
                relay().start()

        forward(own, own_fwd, own_recv, i, j - 1).start()
    for j in range(4):
        landed(own, own_recv, 2 * ((chip + j) % 4) + 1 - core).wait_recv()

    table[0:128, 0:body] = own[:, :, 0:body].reshape(128, body)
    for i in range(8):
        rest = own[i].astype(F32)[12:16, :]
        rest = jnp.concatenate(
            [rest[:, g * tail : (g + 1) * tail] for g in range(3)] + [jnp.zeros((4, tail), F32)], axis=0
        )
        table[i * ROWS : (i + 1) * ROWS, body:points] = rest.astype(BF16)
    grid[...] = jnp.dot(table[:, 0:points], hot[0:points, :], preferred_element_type=F32)

    @pl.when(has_halo)
    def _():
        for q in range(4):
            i = 2 * q + core
            landed(halo, halo_recv, i).wait_recv()
            forward(halo, halo_fwd, halo_recv, i, q).start()
        side_copy().wait_recv()
        for q in range(4):
            landed(halo, halo_recv, 2 * q + 1 - core).wait_recv()

    @pl.when(jnp.logical_not(has_halo))
    def _():
        halo[...] = jnp.zeros_like(halo)
        side_in[...] = jnp.zeros_like(side_in)

    table[0:128, points : points + hbody] = halo[...].reshape(128, hbody)
    for i in range(8):
        rest = halo[i].astype(F32)[12:16, :]
        rest = jnp.concatenate(
            [rest[:, g * htail : (g + 1) * htail] for g in range(3)] + [jnp.zeros((4, htail), F32)],
            axis=0,
        )
        table[i * ROWS : (i + 1) * ROWS, points + hbody : points + send] = rest.astype(BF16)
    rest = side_in[...].astype(F32)
    rest = jnp.concatenate([rest[4 * j : 4 * j + 4, :] for j in range(4)], axis=1)
    rest = jnp.concatenate([rest, jnp.zeros((12, send), F32)], axis=0)
    table[128:144, points : points + send] = rest.astype(BF16)

    values = grid[...] + jnp.dot(
        table[:, points : points + send],
        hot[points : points + send, :],
        preferred_element_type=F32,
    )
    pre = jnp.dot(w_pre[...], values.astype(BF16), preferred_element_type=F32)
    h1 = gelu(pre.astype(BF16).astype(F32) + node[...]).astype(BF16)
    h2 = jnp.dot(hidden_weight[...], h1, preferred_element_type=F32)
    h2 = gelu(h2 + jnp.concatenate([wide[0:80, :]] * 16, axis=1)).astype(BF16)
    kappa = jnp.dot(w_out[...], h2, preferred_element_type=F32)
    kappa = kappa + jnp.concatenate([wide[80:208, :]] * 16, axis=1)
    prod = kappa * values[0:128, :]

    lane8 = iota((8, 8, 128), 2)
    lane1 = iota((1, 128), 1)
    low_at = c * 16
    high_at = (c + 4) % 8 * 16
    acc = jnp.zeros((8, 8, 128), F32)
    number = jnp.ones((1, 128), F32)
    for n in range(16):
        at = slice(n * 128, (n + 1) * 128)
        total = jnp.sum(prod[:, at], axis=1, keepdims=True).reshape(8, ROWS, 1)
        acc = jnp.where(
            lane8 == low_at + n,
            total[:, 0:8],
            jnp.where(lane8 == high_at + n, total[:, 8:16], acc),
        )
        used = jnp.sum(values[128:136, at], axis=1, keepdims=True)[3:4]
        number = jnp.where((lane1 == low_at + n) | (lane1 == high_at + n), used, number)
    res[...] = acc / number[None]

    def res_copy(j):
        target = (c + j) % 8
        return remote(res.at[target], rcv.at[c], res_send.at[j - 1], res_recv.at[c], (s, target))

    for j in range(1, 8):
        res_copy(j).start()
    rcv[c] = res[c]

    for j in range(4):
        when_own(j, lambda copy: copy.wait_send())
    for j in range(1, 4):
        forward(own, own_fwd, own_recv, c, j - 1).wait_send()

    @pl.when(inner)
    def _():
        relay().wait_send()

    @pl.when(has_up)
    def _():
        for q in range(2):
            halo_copy(1, q).wait_send()

    @pl.when(has_down)
    def _():
        for q in range(2):
            halo_copy(0, q).wait_send()

    @pl.when(sends_side)
    def _():
        side_copy().wait_send()

    @pl.when(has_halo)
    def _():
        for q in range(4):
            forward(halo, halo_fwd, halo_recv, 2 * q + core, q).wait_send()

    for j in range(1, 8):
        landed(rcv, res_recv, (c + j) % 8).wait_recv()
    for j in range(1, 8):
        res_copy(j).wait_send()
    group = iota((8, 128), 1) // 16
    lower_rows = jnp.zeros((8, 128), F32)
    upper_rows = jnp.zeros((8, 128), F32)
    for i in range(8):
        lower_rows = jnp.where(group == i, rcv[i], lower_rows)
        upper_rows = jnp.where(group == (i + 4) % 8, rcv[i], upper_rows)
    out[0:8, :] = lower_rows
    out[8:12, :] = pltpu.roll(upper_rows, 64, 1)[0:4, :]


def shards(
    slabs,
    features,
    coords,
    send_rows,
    send_count,
    neighbours,
    neighbour_count,
    geom_weight,
    feat_weight,
    bias_one,
    hidden_weight,
    bias_two,
    out_weight,
    bias_three,
):
    points = features.shape[1]
    send = send_rows.shape[1]
    pairs = 16 * neighbours.shape[1]
    args = (
        features,
        coords,
        send_rows,
        send_count.reshape(2),
        neighbours,
        neighbour_count,
        geom_weight.T,
        feat_weight,
        bias_one.reshape(1, -1),
        hidden_weight,
        bias_two.reshape(1, -1),
        out_weight.T,
        bias_three.reshape(1, -1),
    )
    dma = pltpu.SemaphoreType.DMA
    held = [
        (pltpu.SMEM if i in (3, 5) else pltpu.VMEM)(a.shape, a.dtype) for i, a in enumerate(args)
    ]
    return pl.pallas_call(
        functools.partial(kernel, slabs),
        out_shape=jax.ShapeDtypeStruct((12, 128), F32),
        in_specs=[pl.BlockSpec(memory_space=pl.ANY)] * len(args),
        out_specs=pl.BlockSpec(memory_space=pltpu.VMEM),
        scratch_shapes=held
        + [
            pltpu.VMEM((8, ROWS, points * 3 // 4), BF16),
            pltpu.VMEM((8, ROWS, send * 3 // 4), BF16),
            pltpu.VMEM((2, ROWS, send * 3 // 4), BF16),
            pltpu.VMEM((ROWS, send // 4), BF16),
            pltpu.VMEM((ROWS, send // 4), BF16),
            pltpu.VMEM((9 * ROWS, points + send), BF16),
            pltpu.VMEM((points + send, pairs), BF16),
            pltpu.VMEM((9 * ROWS, pairs), F32),
            pltpu.VMEM((80, pairs), F32),
            pltpu.VMEM((ROWS, points), F32),
            pltpu.VMEM((ROWS, points * 3 // 4), F32),
            pltpu.VMEM((128, 128), F32),
            pltpu.VMEM((208, 128), F32),
            pltpu.VMEM((80, 9 * ROWS), BF16),
            pltpu.VMEM((128, 80), BF16),
            pltpu.VMEM((8, 8, 128), F32),
            pltpu.VMEM((8, 8, 128), F32),
            dma((len(args),)),
            dma((4,)),
            dma((8,)),
            dma((3,)),
            dma((1,)),
            dma((2, 2)),
            dma((8,)),
            dma((4,)),
            dma((1,)),
            dma((1,)),
            dma((7,)),
            dma((8,)),
        ],
        compiler_params=pltpu.CompilerParams(
            collective_id=0, has_side_effects=True, vmem_limit_bytes=60 * 2**20
        ),
    )(*args)


def solution(mesh):
    placed = (
        P("chan", "slab"),
        P(None, "slab"),
        P(None, "slab"),
        P(None, "slab"),
        P("slab", None),
        P("slab"),
        P(),
        P(),
        P(),
        P(),
        P(),
        P(),
        P(),
    )
    return jax.shard_map(
        functools.partial(shards, mesh.shape["slab"]),
        mesh=mesh,
        in_specs=placed,
        out_specs=P("chan", "slab"),
        check_vma=False,
    )
```

```python
import functools

import jax
import jax.numpy as jnp
from jax import lax
from jax.experimental import pallas as pl
from jax.experimental.pallas import tpu as pltpu
from jax.sharding import PartitionSpec as P

MESH = pl.DeviceIdType.MESH
ZD = 2
GX = 16
GY = 4
F32 = jnp.float32
BF16 = jnp.bfloat16
ROWS = 16
BLK = 256
C0 = 0.7978845608028654
C1 = 0.7978845608028654 * 0.044715


def gelu(x):
    half = 0.5 * x
    return half + half * jnp.tanh(x * (C0 + C1 * (x * x)))


def iota(shape, dim):
    return lax.broadcasted_iota(jnp.int32, shape, dim)


def one_hot(index, ramp):
    row = jnp.broadcast_to(index, (16, index.shape[1])).astype(BF16)
    full = jnp.concatenate([row] * (BLK // 16), axis=0)
    return jnp.where(ramp == full, jnp.ones_like(full), jnp.zeros_like(full))


def kernel(
    slabs,
    feat_h,
    coords_h,
    send_rows_h,
    send_count_h,
    nbr_h,
    counts_h,
    geom_h,
    feat_weight_h,
    bias_one_h,
    hidden_weight_h,
    bias_two_h,
    out_weight_h,
    bias_three_h,
    out,
    feat,
    coords,
    send_rows,
    send_count,
    nbr,
    counts,
    geom_t,
    feat_weight,
    bias_one,
    hidden_weight,
    bias_two,
    out_t,
    bias_three,
    own,
    halo,
    picked,
    side_out,
    side_in,
    table,
    hot,
    grid,
    node,
    stage,
    pack,
    small,
    wide,
    w_pre,
    w_out,
    res,
    rcv,
    in_sem,
    own_send,
    own_recv,
    own_fwd,
    halo_send,
    halo_recv,
    halo_fwd,
    side_send,
    side_recv,
    res_send,
    res_recv,
):
    s = lax.axis_index("slab")
    c = lax.axis_index("chan")
    chip = c // 2
    core = c % 2
    sib = c + 1 - 2 * core
    ends = 1 - (chip + 1) // 2 % 2
    half = s * 2 // slabs
    upper = jnp.where(half == 0, ends, 1 - ends)
    rank = 2 * jnp.where(ends == 1, chip // 3, chip - 1) + core
    place = 4 * upper + rank
    has_up = s < slabs - 1
    has_down = s > 0
    has_halo = jnp.where(upper == 1, s < slabs - 1, s > 0)
    source_slab = s - 1 + 2 * upper
    distant = source_slab * 2 // slabs != half
    points = feat.shape[1]
    send = send_rows.shape[1]
    body = points * 3 // 4
    tail = points - body
    hbody = send * 3 // 4
    htail = send - hbody
    pairs = node.shape[1]

    barrier = pltpu.get_barrier_semaphore()
    for j in range(1, 8):
        pl.semaphore_signal(barrier, inc=1, device_id=(s, (c + j) % 8), device_id_type=MESH)

    @pl.when(has_halo)
    def _():
        for q in range(4):
            pl.semaphore_signal(
                barrier, inc=1, device_id=(source_slab, 2 * q + core), device_id_type=MESH
            )

    loads = [
        pltpu.make_async_copy(a, b, in_sem.at[i])
        for i, (a, b) in enumerate(
            [
                (feat_h, feat),
                (coords_h, coords),
                (send_rows_h, send_rows),
                (send_count_h, send_count),
                (nbr_h, nbr),
                (counts_h, counts),
                (geom_h, geom_t),
                (feat_weight_h, feat_weight),
                (bias_one_h, bias_one),
                (hidden_weight_h, hidden_weight),
                (bias_two_h, bias_two),
                (out_weight_h, out_t),
                (bias_three_h, bias_three),
            ]
        )
    ]
    for load in loads:
        load.start()
    for load in loads[:4]:
        load.wait()

    values = feat[...].astype(F32)
    pack[0:12, :] = values[:, 0:body]
    for g in range(3):
        pack[12:16, g * tail : (g + 1) * tail] = values[4 * g : 4 * g + 4, body:points]
    own[c] = pack[...].astype(BF16)

    stage[0:12, :] = values
    stage[12:15, :] = coords[...].astype(F32)
    stage[15:16, :] = jnp.ones((1, points), F32)
    slot = stage[...].astype(BF16)

    ramp = iota((BLK, 128), 0).astype(F32).astype(BF16)
    pieces = points // BLK
    stacked = jnp.concatenate([slot[:, h * BLK : (h + 1) * BLK] for h in range(pieces)], axis=0)
    for d in range(2):
        idx = send_rows[d : d + 1, :]
        idx = jnp.where(iota((1, send), 1) < send_count[d], idx, -1)
        low = (idx & (BLK - 1)).astype(F32)
        high = lax.shift_right_arithmetic(idx, 8)
        hots = jnp.concatenate(
            [one_hot(low[:, t * 128 : (t + 1) * 128], ramp) for t in range(send // 128)], axis=1
        )
        parts = jnp.dot(stacked, hots, preferred_element_type=F32)
        total = jnp.zeros((ROWS, send), F32)
        for h in range(pieces):
            total = total + jnp.where(high == h, parts[h * ROWS : (h + 1) * ROWS], 0.0)
        pack[0:12, 0:hbody] = total[0:12, 0:hbody]
        for g in range(3):
            pack[12:16, g * htail : (g + 1) * htail] = total[4 * g : 4 * g + 4, hbody:send]
        picked[d] = pack[:, 0:hbody].astype(BF16)
        for j in range(4):
            pack[4 * j : 4 * j + 4, 0:htail] = total[12:16, j * htail : (j + 1) * htail]
        side_out[d] = pack[:, 0:htail].astype(BF16)

    pl.semaphore_wait(barrier, 7 + 2 * jnp.where(has_up, 1, 0) + 2 * jnp.where(has_down, 1, 0))

    def remote(src, dst, sem_out, sem_in, target):
        return pltpu.make_async_remote_copy(
            src_ref=src,
            dst_ref=dst,
            send_sem=sem_out,
            recv_sem=sem_in,
            device_id=target,
            device_id_type=MESH,
        )

    def reached(d):
        if d == 1:
            return jnp.where(s + 1 < slabs // 2, 0, 1)
        return jnp.where(s - 1 < slabs // 2, 1, 0)

    def halo_copy(d, q):
        there = jnp.where(reached(d) == 1, 3 * q, 1 + q)
        target = (s - 1 + 2 * d, 2 * there + core)
        return remote(picked.at[d], halo.at[c], halo_send.at[d, q], halo_recv.at[c], target)

    def side_copy(d):
        return remote(
            side_out.at[d], side_in, side_send.at[d], side_recv.at[0], (s - 1 + 2 * d, c)
        )

    def there_of(j):
        up = j - 1 + jnp.where(chip <= j - 1, 1, 0)
        down = 4 - j - jnp.where(3 - chip <= j - 1, 1, 0)
        return jnp.where(chip < 2, down, up)

    def own_copy(j):
        target = sib if j == 0 else 2 * there_of(j) + core
        return remote(own.at[c], own.at[c], own_send.at[j], own_recv.at[c], (s, target))

    def when_list(d, act):
        @pl.when(has_up if d == 1 else has_down)
        def _():
            for q in range(2):
                act(halo_copy(d, q))

            @pl.when(reached(d) == ends)
            def _():
                act(side_copy(d))

    for d in (1, 0):
        when_list(d, lambda copy: copy.start())
    for j in (1, 2, 3, 0):
        own_copy(j).start()

    for load in loads[4:]:
        load.wait()
    small[...] = jnp.zeros_like(small)
    small[0:6, 0:80] = geom_t[...].astype(F32)
    small[6:7, 0:80] = bias_one[...]
    small[7:8, 0:80] = bias_two[...]
    lane = iota((96, 128), 1)
    spread = jnp.where(
        (lane // ROWS * 12 + lane % ROWS == iota((96, 128), 0)) & (lane % ROWS < 12), 1.0, 0.0
    )
    small[8:16, :] = jnp.dot(
        jnp.broadcast_to(bias_three[...], (8, 96)),
        spread,
        preferred_element_type=F32,
        precision=lax.Precision.HIGHEST,
    )
    cols = jnp.transpose(small[...])
    spread = spread.astype(BF16)
    w_pre[:, 0:128] = jnp.dot(feat_weight[...], spread, preferred_element_type=F32).astype(BF16)
    lane16 = iota((80, 16), 1)
    w_side = jnp.zeros((80, 16), F32)
    for i in range(3):
        w_side = jnp.where(lane16 == i, cols[0:80, 3 + i : 4 + i], w_side)
    w_pre[:, 128:144] = w_side.astype(BF16)
    small[0:80, :] = jnp.dot(out_t[...], spread, preferred_element_type=F32)
    w_out[...] = jnp.transpose(small[...])[:, 0:80].astype(BF16)
    along_y = ((rank % GY).astype(F32) + 0.5) / GY
    along_z = ((2 * s + upper).astype(F32) + 0.5) / (ZD * slabs)
    wide[0:80, :] = jnp.broadcast_to(cols[0:80, 7:8], (80, 128))
    wide[80:208, :] = jnp.broadcast_to(cols[:, 8:9], (128, 128))
    slope = jnp.broadcast_to(cols[0:80, 0:1], (80, 128))
    base = jnp.broadcast_to(
        cols[0:80, 1:2] * along_y + cols[0:80, 2:3] * along_z + cols[0:80, 6:7], (80, 128)
    )
    for n in range(16):
        node[:, n * 128 : (n + 1) * 128] = base + slope * ((n + 0.5) / GX)

    first = pl.multiple_of(place * 16, 16)
    idx = nbr[pl.ds(first, 16), :]
    idx = idx - jnp.where(idx >= points, send * upper, 0)
    slots = iota((1, 128), 1)
    rows = []
    for n in range(16):
        rows.append(jnp.where(slots < counts[first + n], idx[n : n + 1, :], -1))
    lows = [(r & (BLK - 1)).astype(F32) for r in rows]
    highs = [lax.shift_right_arithmetic(r, 8) for r in rows]

    def build(kb, carry):
        at = pl.ds(pl.multiple_of(kb * BLK, BLK), BLK)
        for n in range(16):
            pick = jnp.where(highs[n] == kb, lows[n], -1.0)
            hot[at, n * 128 : (n + 1) * 128] = one_hot(pick, ramp)
        return carry

    lax.fori_loop(0, (points + send) // BLK, build, 0)
    extra = jnp.concatenate(
        [coords[...].astype(F32), jnp.ones((1, points), F32), jnp.zeros((12, points), F32)], axis=0
    )
    table[128:144, 0:points] = extra.astype(BF16)

    def landed(buf, sem, i):
        return remote(buf.at[i], buf.at[i], sem.at[i], sem.at[i], (s, sib))

    def forward(buf, fwd, recv, i, k):
        return remote(buf.at[i], buf.at[i], fwd.at[k], recv.at[i], (s, sib))

    def take_halo():
        for q in range(4):
            i = 2 * q + core
            landed(halo, halo_recv, i).wait_recv()
            forward(halo, halo_fwd, halo_recv, i, q).start()

    for j in range(1, 4):
        i = 2 * ((chip + j) % 4) + core
        landed(own, own_recv, i).wait_recv()
        forward(own, own_fwd, own_recv, i, j - 1).start()

    @pl.when(has_halo & jnp.logical_not(distant))
    def _():
        take_halo()

    for j in range(4):
        landed(own, own_recv, 2 * ((chip + j) % 4) + 1 - core).wait_recv()

    table[0:128, 0:body] = own[:, :, 0:body].reshape(128, body)
    for i in range(8):
        rest = own[i].astype(F32)[12:16, :]
        rest = jnp.concatenate(
            [rest[:, g * tail : (g + 1) * tail] for g in range(3)] + [jnp.zeros((4, tail), F32)], axis=0
        )
        table[i * ROWS : (i + 1) * ROWS, body:points] = rest.astype(BF16)
    grid[...] = jnp.dot(table[:, 0:points], hot[0:points, :], preferred_element_type=F32)

    @pl.when(has_halo & distant)
    def _():
        take_halo()

    @pl.when(has_halo)
    def _():
        side_copy(0).wait_recv()
        for q in range(4):
            landed(halo, halo_recv, 2 * q + 1 - core).wait_recv()

    @pl.when(jnp.logical_not(has_halo))
    def _():
        halo[...] = jnp.zeros_like(halo)
        side_in[...] = jnp.zeros_like(side_in)

    table[0:128, points : points + hbody] = halo[...].reshape(128, hbody)
    for i in range(8):
        rest = halo[i].astype(F32)[12:16, :]
        rest = jnp.concatenate(
            [rest[:, g * htail : (g + 1) * htail] for g in range(3)] + [jnp.zeros((4, htail), F32)],
            axis=0,
        )
        table[i * ROWS : (i + 1) * ROWS, points + hbody : points + send] = rest.astype(BF16)
    rest = side_in[...].astype(F32)
    rest = jnp.concatenate([rest[4 * j : 4 * j + 4, :] for j in range(4)], axis=1)
    rest = jnp.concatenate([rest, jnp.zeros((12, send), F32)], axis=0)
    table[128:144, points : points + send] = rest.astype(BF16)

    values = grid[...] + jnp.dot(
        table[:, points : points + send],
        hot[points : points + send, :],
        preferred_element_type=F32,
    )
    pre = jnp.dot(w_pre[...], values.astype(BF16), preferred_element_type=F32)
    h1 = gelu(pre.astype(BF16).astype(F32) + node[...]).astype(BF16)
    h2 = jnp.dot(hidden_weight[...], h1, preferred_element_type=F32)
    h2 = gelu(h2 + jnp.concatenate([wide[0:80, :]] * 16, axis=1)).astype(BF16)
    kappa = jnp.dot(w_out[...], h2, preferred_element_type=F32)
    kappa = kappa + jnp.concatenate([wide[80:208, :]] * 16, axis=1)
    prod = kappa * values[0:128, :]

    lane8 = iota((8, 8, 128), 2)
    lane1 = iota((1, 128), 1)
    low_at = place * 16
    high_at = (place + 4) % 8 * 16
    acc = jnp.zeros((8, 8, 128), F32)
    number = jnp.ones((1, 128), F32)
    for n in range(16):
        at = slice(n * 128, (n + 1) * 128)
        total = jnp.sum(prod[:, at], axis=1, keepdims=True).reshape(8, ROWS, 1)
        acc = jnp.where(
            lane8 == low_at + n,
            total[:, 0:8],
            jnp.where(lane8 == high_at + n, total[:, 8:16], acc),
        )
        used = jnp.sum(values[128:136, at], axis=1, keepdims=True)[3:4]
        number = jnp.where((lane1 == low_at + n) | (lane1 == high_at + n), used, number)
    res[...] = acc / number[None]

    def res_copy(j):
        target = (c + j) % 8
        return remote(
            res.at[target], rcv.at[place], res_send.at[j - 1], res_recv.at[place], (s, target)
        )

    for j in range(1, 8):
        res_copy(j).start()
    rcv[place] = res[c]

    for j in range(4):
        own_copy(j).wait_send()
    for j in range(1, 4):
        forward(own, own_fwd, own_recv, c, j - 1).wait_send()
    for d in (1, 0):
        when_list(d, lambda copy: copy.wait_send())

    @pl.when(has_halo)
    def _():
        for q in range(4):
            forward(halo, halo_fwd, halo_recv, 2 * q + core, q).wait_send()

    for j in range(1, 8):
        landed(rcv, res_recv, (place + j) % 8).wait_recv()
    for j in range(1, 8):
        res_copy(j).wait_send()
    group = iota((8, 128), 1) // 16
    lower_rows = jnp.zeros((8, 128), F32)
    upper_rows = jnp.zeros((8, 128), F32)
    for i in range(8):
        lower_rows = jnp.where(group == i, rcv[i], lower_rows)
        upper_rows = jnp.where(group == (i + 4) % 8, rcv[i], upper_rows)
    out[0:8, :] = lower_rows
    out[8:12, :] = pltpu.roll(upper_rows, 64, 1)[0:4, :]


def shards(
    slabs,
    features,
    coords,
    send_rows,
    send_count,
    neighbours,
    neighbour_count,
    geom_weight,
    feat_weight,
    bias_one,
    hidden_weight,
    bias_two,
    out_weight,
    bias_three,
):
    points = features.shape[1]
    send = send_rows.shape[1]
    pairs = 16 * neighbours.shape[1]
    args = (
        features,
        coords,
        send_rows,
        send_count.reshape(2),
        neighbours,
        neighbour_count,
        geom_weight.T,
        feat_weight,
        bias_one.reshape(1, -1),
        hidden_weight,
        bias_two.reshape(1, -1),
        out_weight.T,
        bias_three.reshape(1, -1),
    )
    dma = pltpu.SemaphoreType.DMA
    held = [
        (pltpu.SMEM if i in (3, 5) else pltpu.VMEM)(a.shape, a.dtype) for i, a in enumerate(args)
    ]
    return pl.pallas_call(
        functools.partial(kernel, slabs),
        out_shape=jax.ShapeDtypeStruct((12, 128), F32),
        in_specs=[pl.BlockSpec(memory_space=pl.ANY)] * len(args),
        out_specs=pl.BlockSpec(memory_space=pltpu.VMEM),
        scratch_shapes=held
        + [
            pltpu.VMEM((8, ROWS, points * 3 // 4), BF16),
            pltpu.VMEM((8, ROWS, send * 3 // 4), BF16),
            pltpu.VMEM((2, ROWS, send * 3 // 4), BF16),
            pltpu.VMEM((2, ROWS, send // 4), BF16),
            pltpu.VMEM((ROWS, send // 4), BF16),
            pltpu.VMEM((9 * ROWS, points + send), BF16),
            pltpu.VMEM((points + send, pairs), BF16),
            pltpu.VMEM((9 * ROWS, pairs), F32),
            pltpu.VMEM((80, pairs), F32),
            pltpu.VMEM((ROWS, points), F32),
            pltpu.VMEM((ROWS, points * 3 // 4), F32),
            pltpu.VMEM((128, 128), F32),
            pltpu.VMEM((208, 128), F32),
            pltpu.VMEM((80, 9 * ROWS), BF16),
            pltpu.VMEM((128, 80), BF16),
            pltpu.VMEM((8, 8, 128), F32),
            pltpu.VMEM((8, 8, 128), F32),
            dma((len(args),)),
            dma((4,)),
            dma((8,)),
            dma((3,)),
            dma((2, 2)),
            dma((8,)),
            dma((4,)),
            dma((2,)),
            dma((1,)),
            dma((7,)),
            dma((8,)),
        ],
        compiler_params=pltpu.CompilerParams(
            collective_id=0, has_side_effects=True, vmem_limit_bytes=60 * 2**20
        ),
    )(*args)


def solution(mesh):
    placed = (
        P("chan", "slab"),
        P(None, "slab"),
        P(None, "slab"),
        P(None, "slab"),
        P("slab", None),
        P("slab"),
        P(),
        P(),
        P(),
        P(),
        P(),
        P(),
        P(),
    )
    return jax.shard_map(
        functools.partial(shards, mesh.shape["slab"]),
        mesh=mesh,
        in_specs=placed,
        out_specs=P("chan", "slab"),
        check_vma=False,
    )
```

```python
import functools

import jax
import jax.numpy as jnp
from jax import lax
from jax.experimental import pallas as pl
from jax.experimental.pallas import tpu as pltpu
from jax.sharding import PartitionSpec as P

MESH = pl.DeviceIdType.MESH
ZD = 2
GX = 16
GY = 4
F32 = jnp.float32
BF16 = jnp.bfloat16
ROWS = 16
BLK = 256
C0 = 0.7978845608028654
C1 = 0.7978845608028654 * 0.044715


def gelu(x):
    half = 0.5 * x
    return half + half * jnp.tanh(x * (C0 + C1 * (x * x)))


def iota(shape, dim):
    return lax.broadcasted_iota(jnp.int32, shape, dim)


def one_hot(index, ramp):
    row = jnp.broadcast_to(index, (16, index.shape[1])).astype(BF16)
    full = jnp.concatenate([row] * (BLK // 16), axis=0)
    return jnp.where(ramp == full, jnp.ones_like(full), jnp.zeros_like(full))


def kernel(
    slabs,
    feat_h,
    coords_h,
    send_rows_h,
    send_count_h,
    nbr_h,
    counts_h,
    geom_h,
    feat_weight_h,
    bias_one_h,
    hidden_weight_h,
    bias_two_h,
    out_weight_h,
    bias_three_h,
    out,
    feat,
    coords,
    send_rows,
    send_count,
    nbr,
    counts,
    geom_t,
    feat_weight,
    bias_one,
    hidden_weight,
    bias_two,
    out_t,
    bias_three,
    own,
    halo,
    picked,
    passing,
    side_out,
    side_in,
    table,
    hot,
    grid,
    node,
    stage,
    pack,
    small,
    wide,
    w_pre,
    w_out,
    res,
    rcv,
    in_sem,
    own_send,
    own_recv,
    own_fwd,
    halo_send,
    far_send,
    halo_recv,
    halo_fwd,
    pass_recv,
    z_send,
    side_send,
    side_recv,
    res_send,
    res_recv,
):
    s = lax.axis_index("slab")
    c = lax.axis_index("chan")
    chip = c // 2
    core = c % 2
    sib = c + 1 - 2 * core
    front = 1 - chip // 2
    half = s * 2 // slabs
    upper = jnp.where(half == 0, front, 1 - front)
    rank = 2 * (chip % 2) + core
    place = 4 * upper + rank
    early = (half == 0) & (front == 1)
    has_up = s < slabs - 1
    has_down = s > 0
    has = (has_down, has_up)
    has_halo = jnp.where(upper == 1, s < slabs - 1, s > 0)
    distant = (s == slabs // 2, s == slabs // 2 - 1)
    near = tuple(has[d] & jnp.logical_not(distant[d]) for d in range(2))
    plane_far = jnp.where(upper == 1, s == slabs // 2 - 1, s == slabs // 2)
    plane_near = has_halo & jnp.logical_not(plane_far)
    flip = 2 * (3 - chip) + core
    beside = 2 * (chip + 1 - 2 * (chip % 2)) + core

    points = feat.shape[1]
    send = send_rows.shape[1]
    body = points * 3 // 4
    tail = points - body
    hbody = send * 3 // 4
    htail = send - hbody
    pairs = node.shape[1]

    barrier = pltpu.get_barrier_semaphore()
    for j in range(1, 8):
        pl.semaphore_signal(barrier, inc=1, device_id=(s, (c + j) % 8), device_id_type=MESH)

    for d in range(2):

        @pl.when(near[d])
        def _():
            pl.semaphore_signal(
                barrier, inc=1, device_id=(s - 1 + 2 * d, c), device_id_type=MESH
            )

        @pl.when(distant[d] & (front == 1))
        def _():
            for q in range(4):
                pl.semaphore_signal(
                    barrier,
                    inc=1,
                    device_id=(s - 1 + 2 * d, 2 * q + core),
                    device_id_type=MESH,
                )

    loads = [
        pltpu.make_async_copy(a, b, in_sem.at[i])
        for i, (a, b) in enumerate(
            [
                (feat_h, feat),
                (coords_h, coords),
                (send_rows_h, send_rows),
                (send_count_h, send_count),
                (nbr_h, nbr),
                (counts_h, counts),
                (geom_h, geom_t),
                (feat_weight_h, feat_weight),
                (bias_one_h, bias_one),
                (hidden_weight_h, hidden_weight),
                (bias_two_h, bias_two),
                (out_weight_h, out_t),
                (bias_three_h, bias_three),
            ]
        )
    ]
    for load in loads:
        load.start()
    for load in loads[:6]:
        load.wait()

    values = feat[...].astype(F32)
    pack[0:12, :] = values[:, 0:body]
    for g in range(3):
        pack[12:16, g * tail : (g + 1) * tail] = values[4 * g : 4 * g + 4, body:points]
    own[c] = pack[...].astype(BF16)

    stage[0:12, :] = values
    stage[12:15, :] = coords[...].astype(F32)
    stage[15:16, :] = jnp.ones((1, points), F32)
    slot = stage[...].astype(BF16)

    ramp = iota((BLK, 128), 0).astype(F32).astype(BF16)
    pieces = points // BLK
    stacked = jnp.concatenate([slot[:, h * BLK : (h + 1) * BLK] for h in range(pieces)], axis=0)
    for d in range(2):
        idx = send_rows[d : d + 1, :]
        idx = jnp.where(iota((1, send), 1) < send_count[d], idx, -1)
        low = (idx & (BLK - 1)).astype(F32)
        high = lax.shift_right_arithmetic(idx, 8)
        hots = jnp.concatenate(
            [one_hot(low[:, t * 128 : (t + 1) * 128], ramp) for t in range(send // 128)], axis=1
        )
        parts = jnp.dot(stacked, hots, preferred_element_type=F32)
        total = jnp.zeros((ROWS, send), F32)
        for h in range(pieces):
            total = total + jnp.where(high == h, parts[h * ROWS : (h + 1) * ROWS], 0.0)
        pack[0:12, 0:hbody] = total[0:12, 0:hbody]
        for g in range(3):
            pack[12:16, g * htail : (g + 1) * htail] = total[4 * g : 4 * g + 4, hbody:send]
        picked[d] = pack[:, 0:hbody].astype(BF16)
        for j in range(4):
            pack[4 * j : 4 * j + 4, 0:htail] = total[12:16, j * htail : (j + 1) * htail]
        side_out[d] = pack[:, 0:htail].astype(BF16)

    first = pl.multiple_of(place * 16, 16)
    idx = nbr[pl.ds(first, 16), :]
    idx = idx - jnp.where(idx >= points, send * upper, 0)
    slots = iota((1, 128), 1)
    rows = []
    for n in range(16):
        rows.append(jnp.where(slots < counts[first + n], idx[n : n + 1, :], -1))
    lows = [(r & (BLK - 1)).astype(F32) for r in rows]
    highs = [lax.shift_right_arithmetic(r, 8) for r in rows]

    def build(kb, carry):
        at = pl.ds(pl.multiple_of(kb * BLK, BLK), BLK)
        for n in range(16):
            pick = jnp.where(highs[n] == kb, lows[n], -1.0)
            hot[at, n * 128 : (n + 1) * 128] = one_hot(pick, ramp)
        return carry

    steps = (points + send) // BLK

    @pl.when(early)
    def _():
        lax.fori_loop(0, steps, build, 0)

    others = [jnp.where(has[d], jnp.where(distant[d], 2, 1), 0) for d in range(2)]
    pl.semaphore_wait(barrier, 7 + others[0] + others[1])

    def remote(src, dst, sem_out, sem_in, target):
        return pltpu.make_async_remote_copy(
            src_ref=src,
            dst_ref=dst,
            send_sem=sem_out,
            recv_sem=sem_in,
            device_id=target,
            device_id_type=MESH,
        )

    def list_copy(d, direct):
        return remote(
            picked.at[d],
            halo.at[c] if direct else passing,
            halo_send.at[d],
            halo_recv.at[c] if direct else pass_recv.at[0],
            (s - 1 + 2 * d, c),
        )

    def far_copy(d, q):
        return remote(
            picked.at[d],
            halo.at[c],
            far_send.at[q],
            halo_recv.at[c],
            (s - 1 + 2 * d, 2 * q + core),
        )

    def side_copy(d, target):
        return remote(
            side_out.at[d], side_in, side_send.at[d], side_recv.at[0], (s - 1 + 2 * d, target)
        )

    def there_of(j):
        up = j - 1 + jnp.where(chip <= j - 1, 1, 0)
        down = 4 - j - jnp.where(3 - chip <= j - 1, 1, 0)
        return jnp.where(chip < 2, down, up)

    def own_copy(j):
        target = sib if j == 0 else 2 * there_of(j) + core
        return remote(own.at[c], own.at[c], own_send.at[j], own_recv.at[c], (s, target))

    def when_list(d, act):
        @pl.when(distant[d])
        def _():
            for q in range(2):
                act(far_copy(d, q))

            @pl.when(front == 0)
            def _():
                act(side_copy(d, flip))

        @pl.when(near[d] & (upper != d))
        def _():
            act(list_copy(d, True))
            act(side_copy(d, c))

        @pl.when(near[d] & (upper == d))
        def _():
            act(list_copy(d, False))

    for d in (1, 0):
        when_list(d, lambda copy: copy.start())
    for j in (1, 2, 3, 0):
        own_copy(j).start()

    def landed(buf, sem, i):
        return remote(buf.at[i], buf.at[i], sem.at[i], sem.at[i], (s, sib))

    def forward(buf, fwd, recv, i, k):
        return remote(buf.at[i], buf.at[i], fwd.at[k], recv.at[i], (s, sib))

    def same_plane():
        return remote(halo.at[c], halo.at[c], z_send.at[0], halo_recv.at[c], (s, beside))

    def other_plane(q):
        return remote(
            passing,
            halo.at[c],
            z_send.at[1 + q],
            halo_recv.at[c],
            (s, 2 * (2 * front + q) + core),
        )

    def when_pass(d, act):
        @pl.when(near[d] & (upper == d))
        def _():
            act(same_plane())

        @pl.when(near[d] & (upper != d))
        def _():
            for q in range(2):
                act(other_plane(q))

    def pass_near():
        for d in range(2):

            @pl.when(near[d] & (upper == d))
            def _():
                landed(halo, halo_recv, c).wait_recv()
                same_plane().start()
                forward(halo, halo_fwd, halo_recv, c, 0).start()

            @pl.when(near[d] & (upper != d))
            def _():
                remote(passing, passing, pass_recv.at[0], pass_recv.at[0], (s, sib)).wait_recv()
                for q in range(2):
                    other_plane(q).start()

    for load in loads[6:]:
        load.wait()
    small[...] = jnp.zeros_like(small)
    small[0:6, 0:80] = geom_t[...].astype(F32)
    small[6:7, 0:80] = bias_one[...]
    small[7:8, 0:80] = bias_two[...]
    lane = iota((96, 128), 1)
    spread = jnp.where(
        (lane // ROWS * 12 + lane % ROWS == iota((96, 128), 0)) & (lane % ROWS < 12), 1.0, 0.0
    )
    small[8:16, :] = jnp.dot(
        jnp.broadcast_to(bias_three[...], (8, 96)),
        spread,
        preferred_element_type=F32,
        precision=lax.Precision.HIGHEST,
    )
    cols = jnp.transpose(small[...])
    spread = spread.astype(BF16)
    w_pre[:, 0:128] = jnp.dot(feat_weight[...], spread, preferred_element_type=F32).astype(BF16)
    lane16 = iota((80, 16), 1)
    w_side = jnp.zeros((80, 16), F32)
    for i in range(3):
        w_side = jnp.where(lane16 == i, cols[0:80, 3 + i : 4 + i], w_side)
    w_pre[:, 128:144] = w_side.astype(BF16)
    small[0:80, :] = jnp.dot(out_t[...], spread, preferred_element_type=F32)
    w_out[...] = jnp.transpose(small[...])[:, 0:80].astype(BF16)
    along_y = ((rank % GY).astype(F32) + 0.5) / GY
    along_z = ((2 * s + upper).astype(F32) + 0.5) / (ZD * slabs)
    wide[0:80, :] = jnp.broadcast_to(cols[0:80, 7:8], (80, 128))
    wide[80:208, :] = jnp.broadcast_to(cols[:, 8:9], (128, 128))
    slope = jnp.broadcast_to(cols[0:80, 0:1], (80, 128))
    base = jnp.broadcast_to(
        cols[0:80, 1:2] * along_y + cols[0:80, 2:3] * along_z + cols[0:80, 6:7], (80, 128)
    )
    for n in range(16):
        node[:, n * 128 : (n + 1) * 128] = base + slope * ((n + 0.5) / GX)

    @pl.when(jnp.logical_not(early))
    def _():
        lax.fori_loop(0, steps // 2, build, 0)

    pass_near()

    @pl.when(jnp.logical_not(early))
    def _():
        lax.fori_loop(steps // 2, steps, build, 0)

    extra = jnp.concatenate(
        [coords[...].astype(F32), jnp.ones((1, points), F32), jnp.zeros((12, points), F32)], axis=0
    )
    table[128:144, 0:points] = extra.astype(BF16)

    for j in range(1, 4):
        i = 2 * ((chip + j) % 4) + core
        landed(own, own_recv, i).wait_recv()
        forward(own, own_fwd, own_recv, i, j - 1).start()

    @pl.when(plane_near)
    def _():
        for q in range(1, 4):
            i = 2 * ((chip + q) % 4) + core
            landed(halo, halo_recv, i).wait_recv()
            forward(halo, halo_fwd, halo_recv, i, q).start()

    for j in range(4):
        landed(own, own_recv, 2 * ((chip + j) % 4) + 1 - core).wait_recv()

    table[0:128, 0:body] = own[:, :, 0:body].reshape(128, body)
    for i in range(8):
        rest = own[i].astype(F32)[12:16, :]
        rest = jnp.concatenate(
            [rest[:, g * tail : (g + 1) * tail] for g in range(3)] + [jnp.zeros((4, tail), F32)], axis=0
        )
        table[i * ROWS : (i + 1) * ROWS, body:points] = rest.astype(BF16)
    grid[...] = jnp.dot(table[:, 0:points], hot[0:points, :], preferred_element_type=F32)

    @pl.when(plane_far)
    def _():
        for q in range(4):
            i = 2 * (3 - q) + core
            landed(halo, halo_recv, i).wait_recv()
            forward(halo, halo_fwd, halo_recv, i, q).start()

    @pl.when(has_halo)
    def _():
        side_copy(0, c).wait_recv()
        for q in range(4):
            landed(halo, halo_recv, 2 * q + 1 - core).wait_recv()

    @pl.when(jnp.logical_not(has_halo))
    def _():
        halo[...] = jnp.zeros_like(halo)
        side_in[...] = jnp.zeros_like(side_in)

    table[0:128, points : points + hbody] = halo[...].reshape(128, hbody)
    for i in range(8):
        rest = halo[i].astype(F32)[12:16, :]
        rest = jnp.concatenate(
            [rest[:, g * htail : (g + 1) * htail] for g in range(3)] + [jnp.zeros((4, htail), F32)],
            axis=0,
        )
        table[i * ROWS : (i + 1) * ROWS, points + hbody : points + send] = rest.astype(BF16)
    rest = side_in[...].astype(F32)
    rest = jnp.concatenate([rest[4 * j : 4 * j + 4, :] for j in range(4)], axis=1)
    rest = jnp.concatenate([rest, jnp.zeros((12, send), F32)], axis=0)
    table[128:144, points : points + send] = rest.astype(BF16)

    values = grid[...] + jnp.dot(
        table[:, points : points + send],
        hot[points : points + send, :],
        preferred_element_type=F32,
    )
    pre = jnp.dot(w_pre[...], values.astype(BF16), preferred_element_type=F32)
    h1 = gelu(pre.astype(BF16).astype(F32) + node[...]).astype(BF16)
    h2 = jnp.dot(hidden_weight[...], h1, preferred_element_type=F32)
    h2 = gelu(h2 + jnp.concatenate([wide[0:80, :]] * 16, axis=1)).astype(BF16)
    kappa = jnp.dot(w_out[...], h2, preferred_element_type=F32)
    kappa = kappa + jnp.concatenate([wide[80:208, :]] * 16, axis=1)
    prod = kappa * values[0:128, :]

    lane8 = iota((8, 8, 128), 2)
    lane1 = iota((1, 128), 1)
    low_at = place * 16
    high_at = (place + 4) % 8 * 16
    acc = jnp.zeros((8, 8, 128), F32)
    number = jnp.ones((1, 128), F32)
    for n in range(16):
        at = slice(n * 128, (n + 1) * 128)
        total = jnp.sum(prod[:, at], axis=1, keepdims=True).reshape(8, ROWS, 1)
        acc = jnp.where(
            lane8 == low_at + n,
            total[:, 0:8],
            jnp.where(lane8 == high_at + n, total[:, 8:16], acc),
        )
        used = jnp.sum(values[128:136, at], axis=1, keepdims=True)[3:4]
        number = jnp.where((lane1 == low_at + n) | (lane1 == high_at + n), used, number)
    res[...] = acc / number[None]

    def res_copy(j):
        target = (c + j) % 8
        return remote(
            res.at[target], rcv.at[place], res_send.at[j - 1], res_recv.at[place], (s, target)
        )

    for j in range(1, 8):
        res_copy(j).start()
    rcv[place] = res[c]

    for j in range(4):
        own_copy(j).wait_send()
    for j in range(1, 4):
        forward(own, own_fwd, own_recv, c, j - 1).wait_send()
    for d in (1, 0):
        when_list(d, lambda copy: copy.wait_send())

    for d in range(2):
        when_pass(d, lambda copy: copy.wait_send())

    @pl.when(has_halo)
    def _():
        for q in range(4):
            forward(halo, halo_fwd, halo_recv, 2 * q + core, q).wait_send()

    for j in range(1, 8):
        landed(rcv, res_recv, (place + j) % 8).wait_recv()
    for j in range(1, 8):
        res_copy(j).wait_send()
    group = iota((8, 128), 1) // 16
    lower_rows = jnp.zeros((8, 128), F32)
    upper_rows = jnp.zeros((8, 128), F32)
    for i in range(8):
        lower_rows = jnp.where(group == i, rcv[i], lower_rows)
        upper_rows = jnp.where(group == (i + 4) % 8, rcv[i], upper_rows)
    out[0:8, :] = lower_rows
    out[8:12, :] = pltpu.roll(upper_rows, 64, 1)[0:4, :]


def shards(
    slabs,
    features,
    coords,
    send_rows,
    send_count,
    neighbours,
    neighbour_count,
    geom_weight,
    feat_weight,
    bias_one,
    hidden_weight,
    bias_two,
    out_weight,
    bias_three,
):
    points = features.shape[1]
    send = send_rows.shape[1]
    pairs = 16 * neighbours.shape[1]
    args = (
        features,
        coords,
        send_rows,
        send_count.reshape(2),
        neighbours,
        neighbour_count,
        geom_weight.T,
        feat_weight,
        bias_one.reshape(1, -1),
        hidden_weight,
        bias_two.reshape(1, -1),
        out_weight.T,
        bias_three.reshape(1, -1),
    )
    dma = pltpu.SemaphoreType.DMA
    held = [
        (pltpu.SMEM if i in (3, 5) else pltpu.VMEM)(a.shape, a.dtype) for i, a in enumerate(args)
    ]
    return pl.pallas_call(
        functools.partial(kernel, slabs),
        out_shape=jax.ShapeDtypeStruct((12, 128), F32),
        in_specs=[pl.BlockSpec(memory_space=pl.ANY)] * len(args),
        out_specs=pl.BlockSpec(memory_space=pltpu.VMEM),
        scratch_shapes=held
        + [
            pltpu.VMEM((8, ROWS, points * 3 // 4), BF16),
            pltpu.VMEM((8, ROWS, send * 3 // 4), BF16),
            pltpu.VMEM((2, ROWS, send * 3 // 4), BF16),
            pltpu.VMEM((ROWS, send * 3 // 4), BF16),
            pltpu.VMEM((2, ROWS, send // 4), BF16),
            pltpu.VMEM((ROWS, send // 4), BF16),
            pltpu.VMEM((9 * ROWS, points + send), BF16),
            pltpu.VMEM((points + send, pairs), BF16),
            pltpu.VMEM((9 * ROWS, pairs), F32),
            pltpu.VMEM((80, pairs), F32),
            pltpu.VMEM((ROWS, points), F32),
            pltpu.VMEM((ROWS, points * 3 // 4), F32),
            pltpu.VMEM((128, 128), F32),
            pltpu.VMEM((208, 128), F32),
            pltpu.VMEM((80, 9 * ROWS), BF16),
            pltpu.VMEM((128, 80), BF16),
            pltpu.VMEM((8, 8, 128), F32),
            pltpu.VMEM((8, 8, 128), F32),
            dma((len(args),)),
            dma((4,)),
            dma((8,)),
            dma((3,)),
            dma((2,)),
            dma((2,)),
            dma((8,)),
            dma((4,)),
            dma((1,)),
            dma((3,)),
            dma((2,)),
            dma((1,)),
            dma((7,)),
            dma((8,)),
        ],
        compiler_params=pltpu.CompilerParams(
            collective_id=0, has_side_effects=True, vmem_limit_bytes=60 * 2**20
        ),
    )(*args)


def solution(mesh):
    placed = (
        P("chan", "slab"),
        P(None, "slab"),
        P(None, "slab"),
        P(None, "slab"),
        P("slab", None),
        P("slab"),
        P(),
        P(),
        P(),
        P(),
        P(),
        P(),
        P(),
    )
    return jax.shard_map(
        functools.partial(shards, mesh.shape["slab"]),
        mesh=mesh,
        in_specs=placed,
        out_specs=P("chan", "slab"),
        check_vma=False,
    )
```

```python
import functools

import jax
import jax.numpy as jnp
from jax import lax
from jax.experimental import pallas as pl
from jax.experimental.pallas import tpu as pltpu
from jax.sharding import PartitionSpec as P

MESH = pl.DeviceIdType.MESH
ZD = 2
GX = 16
GY = 4
F32 = jnp.float32
BF16 = jnp.bfloat16
ROWS = 16
BLK = 256
C0 = 0.7978845608028654
C1 = 0.7978845608028654 * 0.044715


def gelu(x):
    half = 0.5 * x
    return half + half * jnp.tanh(x * (C0 + C1 * (x * x)))


def iota(shape, dim):
    return lax.broadcasted_iota(jnp.int32, shape, dim)


def one_hot(index, ramp):
    row = jnp.broadcast_to(index, (16, index.shape[1])).astype(BF16)
    full = jnp.concatenate([row] * (BLK // 16), axis=0)
    return jnp.where(ramp == full, jnp.ones_like(full), jnp.zeros_like(full))


def kernel(
    slabs,
    feat_h,
    coords_h,
    send_rows_h,
    send_count_h,
    nbr_h,
    counts_h,
    geom_h,
    feat_weight_h,
    bias_one_h,
    hidden_weight_h,
    bias_two_h,
    out_weight_h,
    bias_three_h,
    out,
    feat,
    coords,
    send_rows,
    send_count,
    nbr,
    counts,
    geom_t,
    feat_weight,
    bias_one,
    hidden_weight,
    bias_two,
    out_t,
    bias_three,
    own,
    halo,
    picked,
    passing,
    gated,
    side_out,
    side_in,
    table,
    hot,
    grid,
    node,
    stage,
    pack,
    small,
    wide,
    w_pre,
    w_out,
    res,
    rcv,
    in_sem,
    own_send,
    own_recv,
    own_fwd,
    halo_send,
    far_send,
    halo_recv,
    halo_fwd,
    pass_recv,
    z_send,
    gate_recv,
    gate_send,
    side_send,
    side_recv,
    res_send,
    res_recv,
):
    s = lax.axis_index("slab")
    c = lax.axis_index("chan")
    chip = c // 2
    core = c % 2
    sib = c + 1 - 2 * core
    front = 1 - chip // 2
    half = s * 2 // slabs
    upper = jnp.where(half == 0, front, 1 - front)
    rank = 2 * (chip % 2) + core
    place = 4 * upper + rank
    early = (half == 0) & (front == 1)
    has_up = s < slabs - 1
    has_down = s > 0
    has = (has_down, has_up)
    has_halo = jnp.where(upper == 1, s < slabs - 1, s > 0)
    distant = (s == slabs // 2, s == slabs // 2 - 1)
    near = tuple(has[d] & jnp.logical_not(distant[d]) for d in range(2))
    plane_far = jnp.where(upper == 1, s == slabs // 2 - 1, s == slabs // 2)
    plane_near = has_halo & jnp.logical_not(plane_far)
    flip = 2 * (3 - chip) + core
    beside = 2 * (chip + 1 - 2 * (chip % 2)) + core

    points = feat.shape[1]
    send = send_rows.shape[1]
    body = points * 3 // 4
    tail = points - body
    hbody = send * 3 // 4
    htail = send - hbody
    pairs = node.shape[1]

    barrier = pltpu.get_barrier_semaphore()
    for j in range(1, 8):
        pl.semaphore_signal(barrier, inc=1, device_id=(s, (c + j) % 8), device_id_type=MESH)

    for d in range(2):

        @pl.when(near[d])
        def _():
            pl.semaphore_signal(
                barrier, inc=1, device_id=(s - 1 + 2 * d, c), device_id_type=MESH
            )

    def greet(there):
        pl.semaphore_signal(barrier, inc=1, device_id=there, device_id_type=MESH)

    @pl.when(distant[1] & (front == 1))
    def _():
        for q in range(4):
            greet((s + 1, 2 * q + core))

    @pl.when(distant[0] & (chip != 2))
    def _():
        greet((s - 1, 2 * jnp.where(chip == 3, 0, 3) + core))

    @pl.when(distant[0] & ((chip == 0) | (chip == 3)))
    def _():
        greet((s - 1, 2 * jnp.where(chip == 3, 1, 2) + core))

    loads = [
        pltpu.make_async_copy(a, b, in_sem.at[i])
        for i, (a, b) in enumerate(
            [
                (feat_h, feat),
                (coords_h, coords),
                (send_rows_h, send_rows),
                (send_count_h, send_count),
                (nbr_h, nbr),
                (counts_h, counts),
                (geom_h, geom_t),
                (feat_weight_h, feat_weight),
                (bias_one_h, bias_one),
                (hidden_weight_h, hidden_weight),
                (bias_two_h, bias_two),
                (out_weight_h, out_t),
                (bias_three_h, bias_three),
            ]
        )
    ]
    for load in loads:
        load.start()
    for load in loads[:6]:
        load.wait()

    values = feat[...].astype(F32)
    pack[0:12, :] = values[:, 0:body]
    for g in range(3):
        pack[12:16, g * tail : (g + 1) * tail] = values[4 * g : 4 * g + 4, body:points]
    own[c] = pack[...].astype(BF16)

    stage[0:12, :] = values
    stage[12:15, :] = coords[...].astype(F32)
    stage[15:16, :] = jnp.ones((1, points), F32)
    slot = stage[...].astype(BF16)

    ramp = iota((BLK, 128), 0).astype(F32).astype(BF16)
    pieces = points // BLK
    stacked = jnp.concatenate([slot[:, h * BLK : (h + 1) * BLK] for h in range(pieces)], axis=0)
    for d in range(2):
        idx = send_rows[d : d + 1, :]
        idx = jnp.where(iota((1, send), 1) < send_count[d], idx, -1)
        low = (idx & (BLK - 1)).astype(F32)
        high = lax.shift_right_arithmetic(idx, 8)
        hots = jnp.concatenate(
            [one_hot(low[:, t * 128 : (t + 1) * 128], ramp) for t in range(send // 128)], axis=1
        )
        parts = jnp.dot(stacked, hots, preferred_element_type=F32)
        total = jnp.zeros((ROWS, send), F32)
        for h in range(pieces):
            total = total + jnp.where(high == h, parts[h * ROWS : (h + 1) * ROWS], 0.0)
        pack[0:12, 0:hbody] = total[0:12, 0:hbody]
        for g in range(3):
            pack[12:16, g * htail : (g + 1) * htail] = total[4 * g : 4 * g + 4, hbody:send]
        picked[d] = pack[:, 0:hbody].astype(BF16)
        for j in range(4):
            pack[4 * j : 4 * j + 4, 0:htail] = total[12:16, j * htail : (j + 1) * htail]
        side_out[d] = pack[:, 0:htail].astype(BF16)

    first = pl.multiple_of(place * 16, 16)
    idx = nbr[pl.ds(first, 16), :]
    idx = idx - jnp.where(idx >= points, send * upper, 0)
    slots = iota((1, 128), 1)
    rows = []
    for n in range(16):
        rows.append(jnp.where(slots < counts[first + n], idx[n : n + 1, :], -1))
    lows = [(r & (BLK - 1)).astype(F32) for r in rows]
    highs = [lax.shift_right_arithmetic(r, 8) for r in rows]

    def build(kb, carry):
        at = pl.ds(pl.multiple_of(kb * BLK, BLK), BLK)
        for n in range(16):
            pick = jnp.where(highs[n] == kb, lows[n], -1.0)
            hot[at, n * 128 : (n + 1) * 128] = one_hot(pick, ramp)
        return carry

    steps = (points + send) // BLK

    @pl.when(early)
    def _():
        lax.fori_loop(0, steps, build, 0)

    far_count = (2, jnp.where(chip == 3, 2, 1))
    others = [jnp.where(has[d], jnp.where(distant[d], far_count[d], 1), 0) for d in range(2)]
    pl.semaphore_wait(barrier, 7 + others[0] + others[1])

    def remote(src, dst, sem_out, sem_in, target):
        return pltpu.make_async_remote_copy(
            src_ref=src,
            dst_ref=dst,
            send_sem=sem_out,
            recv_sem=sem_in,
            device_id=target,
            device_id_type=MESH,
        )

    def list_copy(d, direct):
        return remote(
            picked.at[d],
            halo.at[c] if direct else passing,
            halo_send.at[d],
            halo_recv.at[c] if direct else pass_recv.at[0],
            (s - 1 + 2 * d, c),
        )

    def far_down(q):
        return remote(
            picked.at[0], halo.at[c], far_send.at[q], halo_recv.at[c], (s - 1, 2 * q + core)
        )

    def far_up():
        return remote(picked.at[1], halo.at[c], far_send.at[0], halo_recv.at[c], (s + 1, core))

    def far_gate(q):
        return remote(
            picked.at[1], gated.at[q], far_send.at[1], gate_recv.at[q], (s + 1, 6 + core)
        )

    def side_copy(d, target, k=0):
        return remote(
            side_out.at[d],
            side_in,
            side_send.at[2 * k + d],
            side_recv.at[0],
            (s - 1 + 2 * d, target),
        )

    def there_of(j):
        up = j - 1 + jnp.where(chip <= j - 1, 1, 0)
        down = 4 - j - jnp.where(3 - chip <= j - 1, 1, 0)
        return jnp.where(chip < 2, down, up)

    def own_copy(j):
        target = sib if j == 0 else 2 * there_of(j) + core
        return remote(own.at[c], own.at[c], own_send.at[j], own_recv.at[c], (s, target))

    def when_list(d, act):
        if d == 1:

            @pl.when(distant[1] & (front == 0))
            def _():
                act(far_up())

            @pl.when(distant[1] & (chip == 3))
            def _():
                act(side_copy(1, core, 0))
                act(side_copy(1, 2 + core, 1))

            for q in range(2):

                @pl.when(distant[1] & (chip == q))
                def _():
                    act(far_gate(q))

        else:

            @pl.when(distant[0])
            def _():
                for q in range(2):
                    act(far_down(q))

            @pl.when(distant[0] & (front == 0))
            def _():
                act(side_copy(0, flip))

        @pl.when(near[d] & (upper != d))
        def _():
            act(list_copy(d, True))
            act(side_copy(d, c))

        @pl.when(near[d] & (upper == d))
        def _():
            act(list_copy(d, False))

    for d in (1, 0):
        when_list(d, lambda copy: copy.start())
    for j in (1, 2, 3, 0):
        own_copy(j).start()

    def landed(buf, sem, i):
        return remote(buf.at[i], buf.at[i], sem.at[i], sem.at[i], (s, sib))

    def forward(buf, fwd, recv, i, k):
        return remote(buf.at[i], buf.at[i], fwd.at[k], recv.at[i], (s, sib))

    def same_plane():
        return remote(halo.at[c], halo.at[c], z_send.at[0], halo_recv.at[c], (s, beside))

    def other_plane(q):
        return remote(
            passing,
            halo.at[c],
            z_send.at[1 + q],
            halo_recv.at[c],
            (s, 2 * (2 * front + q) + core),
        )

    def when_pass(d, act):
        @pl.when(near[d] & (upper == d))
        def _():
            act(same_plane())

        @pl.when(near[d] & (upper != d))
        def _():
            for q in range(2):
                act(other_plane(q))

    def pass_near():
        for d in range(2):

            @pl.when(near[d] & (upper == d))
            def _():
                landed(halo, halo_recv, c).wait_recv()
                same_plane().start()
                forward(halo, halo_fwd, halo_recv, c, 0).start()

            @pl.when(near[d] & (upper != d))
            def _():
                remote(passing, passing, pass_recv.at[0], pass_recv.at[0], (s, sib)).wait_recv()
                for q in range(2):
                    other_plane(q).start()

    for load in loads[6:]:
        load.wait()
    small[...] = jnp.zeros_like(small)
    small[0:6, 0:80] = geom_t[...].astype(F32)
    small[6:7, 0:80] = bias_one[...]
    small[7:8, 0:80] = bias_two[...]
    lane = iota((96, 128), 1)
    spread = jnp.where(
        (lane // ROWS * 12 + lane % ROWS == iota((96, 128), 0)) & (lane % ROWS < 12), 1.0, 0.0
    )
    small[8:16, :] = jnp.dot(
        jnp.broadcast_to(bias_three[...], (8, 96)),
        spread,
        preferred_element_type=F32,
        precision=lax.Precision.HIGHEST,
    )
    cols = jnp.transpose(small[...])
    spread = spread.astype(BF16)
    w_pre[:, 0:128] = jnp.dot(feat_weight[...], spread, preferred_element_type=F32).astype(BF16)
    lane16 = iota((80, 16), 1)
    w_side = jnp.zeros((80, 16), F32)
    for i in range(3):
        w_side = jnp.where(lane16 == i, cols[0:80, 3 + i : 4 + i], w_side)
    w_pre[:, 128:144] = w_side.astype(BF16)
    small[0:80, :] = jnp.dot(out_t[...], spread, preferred_element_type=F32)
    w_out[...] = jnp.transpose(small[...])[:, 0:80].astype(BF16)
    along_y = ((rank % GY).astype(F32) + 0.5) / GY
    along_z = ((2 * s + upper).astype(F32) + 0.5) / (ZD * slabs)
    wide[0:80, :] = jnp.broadcast_to(cols[0:80, 7:8], (80, 128))
    wide[80:208, :] = jnp.broadcast_to(cols[:, 8:9], (128, 128))
    slope = jnp.broadcast_to(cols[0:80, 0:1], (80, 128))
    base = jnp.broadcast_to(
        cols[0:80, 1:2] * along_y + cols[0:80, 2:3] * along_z + cols[0:80, 6:7], (80, 128)
    )
    for n in range(16):
        node[:, n * 128 : (n + 1) * 128] = base + slope * ((n + 0.5) / GX)

    @pl.when(jnp.logical_not(early))
    def _():
        lax.fori_loop(0, steps // 2, build, 0)

    pass_near()

    @pl.when(jnp.logical_not(early))
    def _():
        lax.fori_loop(steps // 2, steps, build, 0)

    extra = jnp.concatenate(
        [coords[...].astype(F32), jnp.ones((1, points), F32), jnp.zeros((12, points), F32)], axis=0
    )
    table[128:144, 0:points] = extra.astype(BF16)

    for j in range(1, 4):
        i = 2 * ((chip + j) % 4) + core
        landed(own, own_recv, i).wait_recv()
        forward(own, own_fwd, own_recv, i, j - 1).start()

    def gate_copy(q, k):
        i = 2 * q + core
        return remote(
            gated.at[q], halo.at[i], gate_send.at[2 * q + k], halo_recv.at[i], (s, 2 * k + core)
        )

    def gate_pass(q):
        i = 2 * q + core
        return remote(
            halo.at[i], halo.at[i], gate_send.at[q - 2], halo_recv.at[i], (s, 2 + core)
        )

    @pl.when(distant[0] & (chip == 3))
    def _():
        for q in range(2):
            remote(gated.at[q], gated.at[q], gate_recv.at[q], gate_recv.at[q], (s, sib)).wait_recv()
            for k in range(2):
                gate_copy(q, k).start()

    @pl.when(distant[0] & (chip == 0))
    def _():
        for q in (3, 2):
            i = 2 * q + core
            landed(halo, halo_recv, i).wait_recv()
            gate_pass(q).start()
            forward(halo, halo_fwd, halo_recv, i, q).start()

    @pl.when(plane_near)
    def _():
        for q in range(1, 4):
            i = 2 * ((chip + q) % 4) + core
            landed(halo, halo_recv, i).wait_recv()
            forward(halo, halo_fwd, halo_recv, i, q).start()

    for j in range(4):
        landed(own, own_recv, 2 * ((chip + j) % 4) + 1 - core).wait_recv()

    table[0:128, 0:body] = own[:, :, 0:body].reshape(128, body)
    for i in range(8):
        rest = own[i].astype(F32)[12:16, :]
        rest = jnp.concatenate(
            [rest[:, g * tail : (g + 1) * tail] for g in range(3)] + [jnp.zeros((4, tail), F32)], axis=0
        )
        table[i * ROWS : (i + 1) * ROWS, body:points] = rest.astype(BF16)
    grid[...] = jnp.dot(table[:, 0:points], hot[0:points, :], preferred_element_type=F32)

    @pl.when(plane_far)
    def _():
        for q in (3, 2, 1, 0):
            i = 2 * q + core

            @pl.when((s < slabs // 2) | (chip == 1) | (q < 2))
            def _():
                landed(halo, halo_recv, i).wait_recv()
                forward(halo, halo_fwd, halo_recv, i, q).start()

    @pl.when(has_halo)
    def _():
        side_copy(0, c).wait_recv()
        for q in range(4):
            landed(halo, halo_recv, 2 * q + 1 - core).wait_recv()

    @pl.when(jnp.logical_not(has_halo))
    def _():
        halo[...] = jnp.zeros_like(halo)
        side_in[...] = jnp.zeros_like(side_in)

    table[0:128, points : points + hbody] = halo[...].reshape(128, hbody)
    for i in range(8):
        rest = halo[i].astype(F32)[12:16, :]
        rest = jnp.concatenate(
            [rest[:, g * htail : (g + 1) * htail] for g in range(3)] + [jnp.zeros((4, htail), F32)],
            axis=0,
        )
        table[i * ROWS : (i + 1) * ROWS, points + hbody : points + send] = rest.astype(BF16)
    rest = side_in[...].astype(F32)
    rest = jnp.concatenate([rest[4 * j : 4 * j + 4, :] for j in range(4)], axis=1)
    rest = jnp.concatenate([rest, jnp.zeros((12, send), F32)], axis=0)
    table[128:144, points : points + send] = rest.astype(BF16)

    values = grid[...] + jnp.dot(
        table[:, points : points + send],
        hot[points : points + send, :],
        preferred_element_type=F32,
    )
    pre = jnp.dot(w_pre[...], values.astype(BF16), preferred_element_type=F32)
    h1 = gelu(pre.astype(BF16).astype(F32) + node[...]).astype(BF16)
    h2 = jnp.dot(hidden_weight[...], h1, preferred_element_type=F32)
    h2 = gelu(h2 + jnp.concatenate([wide[0:80, :]] * 16, axis=1)).astype(BF16)
    kappa = jnp.dot(w_out[...], h2, preferred_element_type=F32)
    kappa = kappa + jnp.concatenate([wide[80:208, :]] * 16, axis=1)
    prod = kappa * values[0:128, :]

    lane8 = iota((8, 8, 128), 2)
    lane1 = iota((1, 128), 1)
    low_at = place * 16
    high_at = (place + 4) % 8 * 16
    acc = jnp.zeros((8, 8, 128), F32)
    number = jnp.ones((1, 128), F32)
    for n in range(16):
        at = slice(n * 128, (n + 1) * 128)
        total = jnp.sum(prod[:, at], axis=1, keepdims=True).reshape(8, ROWS, 1)
        acc = jnp.where(
            lane8 == low_at + n,
            total[:, 0:8],
            jnp.where(lane8 == high_at + n, total[:, 8:16], acc),
        )
        used = jnp.sum(values[128:136, at], axis=1, keepdims=True)[3:4]
        number = jnp.where((lane1 == low_at + n) | (lane1 == high_at + n), used, number)
    res[...] = acc / number[None]

    def res_copy(j):
        target = (c + j) % 8
        return remote(
            res.at[target], rcv.at[place], res_send.at[j - 1], res_recv.at[place], (s, target)
        )

    for j in range(1, 8):
        res_copy(j).start()
    rcv[place] = res[c]

    for j in range(4):
        own_copy(j).wait_send()
    for j in range(1, 4):
        forward(own, own_fwd, own_recv, c, j - 1).wait_send()
    for d in (1, 0):
        when_list(d, lambda copy: copy.wait_send())

    for d in range(2):
        when_pass(d, lambda copy: copy.wait_send())

    @pl.when(distant[0] & (chip == 3))
    def _():
        for q in range(2):
            for k in range(2):
                gate_copy(q, k).wait_send()

    @pl.when(distant[0] & (chip == 0))
    def _():
        for q in (3, 2):
            gate_pass(q).wait_send()

    @pl.when(has_halo)
    def _():
        for q in range(4):
            forward(halo, halo_fwd, halo_recv, 2 * q + core, q).wait_send()

    for j in range(1, 8):
        landed(rcv, res_recv, (place + j) % 8).wait_recv()
    for j in range(1, 8):
        res_copy(j).wait_send()
    group = iota((8, 128), 1) // 16
    lower_rows = jnp.zeros((8, 128), F32)
    upper_rows = jnp.zeros((8, 128), F32)
    for i in range(8):
        lower_rows = jnp.where(group == i, rcv[i], lower_rows)
        upper_rows = jnp.where(group == (i + 4) % 8, rcv[i], upper_rows)
    out[0:8, :] = lower_rows
    out[8:12, :] = pltpu.roll(upper_rows, 64, 1)[0:4, :]


def shards(
    slabs,
    features,
    coords,
    send_rows,
    send_count,
    neighbours,
    neighbour_count,
    geom_weight,
    feat_weight,
    bias_one,
    hidden_weight,
    bias_two,
    out_weight,
    bias_three,
):
    points = features.shape[1]
    send = send_rows.shape[1]
    pairs = 16 * neighbours.shape[1]
    args = (
        features,
        coords,
        send_rows,
        send_count.reshape(2),
        neighbours,
        neighbour_count,
        geom_weight.T,
        feat_weight,
        bias_one.reshape(1, -1),
        hidden_weight,
        bias_two.reshape(1, -1),
        out_weight.T,
        bias_three.reshape(1, -1),
    )
    dma = pltpu.SemaphoreType.DMA
    held = [
        (pltpu.SMEM if i in (3, 5) else pltpu.VMEM)(a.shape, a.dtype) for i, a in enumerate(args)
    ]
    return pl.pallas_call(
        functools.partial(kernel, slabs),
        out_shape=jax.ShapeDtypeStruct((12, 128), F32),
        in_specs=[pl.BlockSpec(memory_space=pl.ANY)] * len(args),
        out_specs=pl.BlockSpec(memory_space=pltpu.VMEM),
        scratch_shapes=held
        + [
            pltpu.VMEM((8, ROWS, points * 3 // 4), BF16),
            pltpu.VMEM((8, ROWS, send * 3 // 4), BF16),
            pltpu.VMEM((2, ROWS, send * 3 // 4), BF16),
            pltpu.VMEM((ROWS, send * 3 // 4), BF16),
            pltpu.VMEM((2, ROWS, send * 3 // 4), BF16),
            pltpu.VMEM((2, ROWS, send // 4), BF16),
            pltpu.VMEM((ROWS, send // 4), BF16),
            pltpu.VMEM((9 * ROWS, points + send), BF16),
            pltpu.VMEM((points + send, pairs), BF16),
            pltpu.VMEM((9 * ROWS, pairs), F32),
            pltpu.VMEM((80, pairs), F32),
            pltpu.VMEM((ROWS, points), F32),
            pltpu.VMEM((ROWS, points * 3 // 4), F32),
            pltpu.VMEM((128, 128), F32),
            pltpu.VMEM((208, 128), F32),
            pltpu.VMEM((80, 9 * ROWS), BF16),
            pltpu.VMEM((128, 80), BF16),
            pltpu.VMEM((8, 8, 128), F32),
            pltpu.VMEM((8, 8, 128), F32),
            dma((len(args),)),
            dma((4,)),
            dma((8,)),
            dma((3,)),
            dma((2,)),
            dma((2,)),
            dma((8,)),
            dma((4,)),
            dma((1,)),
            dma((3,)),
            dma((2,)),
            dma((4,)),
            dma((4,)),
            dma((1,)),
            dma((7,)),
            dma((8,)),
        ],
        compiler_params=pltpu.CompilerParams(
            collective_id=0, has_side_effects=True, vmem_limit_bytes=60 * 2**20
        ),
    )(*args)


def solution(mesh):
    placed = (
        P("chan", "slab"),
        P(None, "slab"),
        P(None, "slab"),
        P(None, "slab"),
        P("slab", None),
        P("slab"),
        P(),
        P(),
        P(),
        P(),
        P(),
        P(),
        P(),
    )
    return jax.shard_map(
        functools.partial(shards, mesh.shape["slab"]),
        mesh=mesh,
        in_specs=placed,
        out_specs=P("chan", "slab"),
        check_vma=False,
    )
```

```python
import functools

import jax
import jax.numpy as jnp
from jax import lax
from jax.experimental import pallas as pl
from jax.experimental.pallas import tpu as pltpu
from jax.sharding import PartitionSpec as P

MESH = pl.DeviceIdType.MESH
ZD = 2
GX = 16
GY = 4
F32 = jnp.float32
BF16 = jnp.bfloat16
ROWS = 16
BLK = 256
C0 = 0.7978845608028654
C1 = 0.7978845608028654 * 0.044715


def gelu(x):
    half = 0.5 * x
    return half + half * jnp.tanh(x * (C0 + C1 * (x * x)))


def iota(shape, dim):
    return lax.broadcasted_iota(jnp.int32, shape, dim)


def one_hot(index, ramp):
    row = jnp.broadcast_to(index, (16, index.shape[1])).astype(BF16)
    full = jnp.concatenate([row] * (BLK // 16), axis=0)
    return jnp.where(ramp == full, jnp.ones_like(full), jnp.zeros_like(full))


def kernel(
    slabs,
    feat_h,
    coords_h,
    send_rows_h,
    send_count_h,
    nbr_h,
    counts_h,
    geom_h,
    feat_weight_h,
    bias_one_h,
    hidden_weight_h,
    bias_two_h,
    out_weight_h,
    bias_three_h,
    out,
    feat,
    coords,
    send_rows,
    send_count,
    nbr,
    counts,
    geom_t,
    feat_weight,
    bias_one,
    hidden_weight,
    bias_two,
    out_t,
    bias_three,
    own,
    halo,
    picked,
    passing,
    side_out,
    side_in,
    table,
    hot,
    grid,
    node,
    stage,
    pack,
    small,
    wide,
    w_pre,
    w_out,
    res,
    rcv,
    in_sem,
    own_send,
    own_recv,
    own_fwd,
    halo_send,
    far_send,
    halo_recv,
    halo_fwd,
    pass_recv,
    z_send,
    side_send,
    side_recv,
    res_send,
    res_recv,
):
    s = lax.axis_index("slab")
    c = lax.axis_index("chan")
    chip = c // 2
    core = c % 2
    sib = c + 1 - 2 * core
    front = 1 - chip // 2
    ends = 1 - (chip + 1) // 2 % 2
    half = s * 2 // slabs
    begins = s == slabs // 2

    def works_upper(slab):
        usual = jnp.where(slab * 2 // slabs == 0, front, 1 - front)
        return jnp.where(slab == slabs // 2, ends, usual)

    upper = works_upper(s)
    rank = 2 * jnp.where(begins, jnp.where(ends == 1, chip // 3, chip - 1), chip % 2) + core
    place = 4 * upper + rank
    early = (half == 0) & (front == 1)
    has_up = s < slabs - 1
    has_down = s > 0
    has = (has_down, has_up)
    has_halo = jnp.where(upper == 1, s < slabs - 1, s > 0)
    distant = (s == slabs // 2, s == slabs // 2 - 1)
    near = tuple(has[d] & jnp.logical_not(distant[d]) for d in range(2))
    plane_far = jnp.where(upper == 1, s == slabs // 2 - 1, s == slabs // 2)
    plane_near = has_halo & jnp.logical_not(plane_far)
    beside = 2 * jnp.where(begins, 3 - chip, chip + 1 - 2 * (chip % 2)) + core

    points = feat.shape[1]
    send = send_rows.shape[1]
    body = points * 3 // 4
    tail = points - body
    hbody = send * 3 // 4
    htail = send - hbody
    pairs = node.shape[1]

    barrier = pltpu.get_barrier_semaphore()
    for j in range(1, 8):
        pl.semaphore_signal(barrier, inc=1, device_id=(s, (c + j) % 8), device_id_type=MESH)

    for d in range(2):

        @pl.when(near[d])
        def _():
            pl.semaphore_signal(
                barrier, inc=1, device_id=(s - 1 + 2 * d, c), device_id_type=MESH
            )

        @pl.when(distant[d] & (upper == d))
        def _():
            for q in range(4):
                pl.semaphore_signal(
                    barrier,
                    inc=1,
                    device_id=(s - 1 + 2 * d, 2 * q + core),
                    device_id_type=MESH,
                )

    loads = [
        pltpu.make_async_copy(a, b, in_sem.at[i])
        for i, (a, b) in enumerate(
            [
                (feat_h, feat),
                (coords_h, coords),
                (send_rows_h, send_rows),
                (send_count_h, send_count),
                (nbr_h, nbr),
                (counts_h, counts),
                (geom_h, geom_t),
                (feat_weight_h, feat_weight),
                (bias_one_h, bias_one),
                (hidden_weight_h, hidden_weight),
                (bias_two_h, bias_two),
                (out_weight_h, out_t),
                (bias_three_h, bias_three),
            ]
        )
    ]
    for load in loads:
        load.start()
    for load in loads[:6]:
        load.wait()

    values = feat[...].astype(F32)
    pack[0:12, :] = values[:, 0:body]
    for g in range(3):
        pack[12:16, g * tail : (g + 1) * tail] = values[4 * g : 4 * g + 4, body:points]
    own[c] = pack[...].astype(BF16)

    stage[0:12, :] = values
    stage[12:15, :] = coords[...].astype(F32)
    stage[15:16, :] = jnp.ones((1, points), F32)
    slot = stage[...].astype(BF16)

    ramp = iota((BLK, 128), 0).astype(F32).astype(BF16)
    pieces = points // BLK
    stacked = jnp.concatenate([slot[:, h * BLK : (h + 1) * BLK] for h in range(pieces)], axis=0)
    for d in range(2):
        idx = send_rows[d : d + 1, :]
        idx = jnp.where(iota((1, send), 1) < send_count[d], idx, -1)
        low = (idx & (BLK - 1)).astype(F32)
        high = lax.shift_right_arithmetic(idx, 8)
        hots = jnp.concatenate(
            [one_hot(low[:, t * 128 : (t + 1) * 128], ramp) for t in range(send // 128)], axis=1
        )
        parts = jnp.dot(stacked, hots, preferred_element_type=F32)
        total = jnp.zeros((ROWS, send), F32)
        for h in range(pieces):
            total = total + jnp.where(high == h, parts[h * ROWS : (h + 1) * ROWS], 0.0)
        pack[0:12, 0:hbody] = total[0:12, 0:hbody]
        for g in range(3):
            pack[12:16, g * htail : (g + 1) * htail] = total[4 * g : 4 * g + 4, hbody:send]
        picked[d] = pack[:, 0:hbody].astype(BF16)
        for j in range(4):
            pack[4 * j : 4 * j + 4, 0:htail] = total[12:16, j * htail : (j + 1) * htail]
        side_out[d] = pack[:, 0:htail].astype(BF16)

    first = pl.multiple_of(place * 16, 16)
    idx = nbr[pl.ds(first, 16), :]
    idx = idx - jnp.where(idx >= points, send * upper, 0)
    slots = iota((1, 128), 1)
    rows = []
    for n in range(16):
        rows.append(jnp.where(slots < counts[first + n], idx[n : n + 1, :], -1))
    lows = [(r & (BLK - 1)).astype(F32) for r in rows]
    highs = [lax.shift_right_arithmetic(r, 8) for r in rows]

    def build(kb, carry):
        at = pl.ds(pl.multiple_of(kb * BLK, BLK), BLK)
        for n in range(16):
            pick = jnp.where(highs[n] == kb, lows[n], -1.0)
            hot[at, n * 128 : (n + 1) * 128] = one_hot(pick, ramp)
        return carry

    steps = (points + send) // BLK

    @pl.when(early)
    def _():
        lax.fori_loop(0, steps, build, 0)

    others = [jnp.where(has[d], jnp.where(distant[d], 2, 1), 0) for d in range(2)]
    pl.semaphore_wait(barrier, 7 + others[0] + others[1])

    def remote(src, dst, sem_out, sem_in, target):
        return pltpu.make_async_remote_copy(
            src_ref=src,
            dst_ref=dst,
            send_sem=sem_out,
            recv_sem=sem_in,
            device_id=target,
            device_id_type=MESH,
        )

    def list_copy(d, direct):
        return remote(
            picked.at[d],
            halo.at[c] if direct else passing,
            halo_send.at[d],
            halo_recv.at[c] if direct else pass_recv.at[0],
            (s - 1 + 2 * d, c),
        )

    def far_copy(d, q):
        return remote(
            picked.at[d],
            halo.at[c],
            far_send.at[q],
            halo_recv.at[c],
            (s - 1 + 2 * d, 2 * (q + d) + core),
        )

    def side_copy(d, target):
        return remote(
            side_out.at[d], side_in, side_send.at[d], side_recv.at[0], (s - 1 + 2 * d, target)
        )

    def there_of(j):
        up = j - 1 + jnp.where(chip <= j - 1, 1, 0)
        down = 4 - j - jnp.where(3 - chip <= j - 1, 1, 0)
        return jnp.where(chip < 2, down, up)

    def own_copy(j):
        target = sib if j == 0 else 2 * there_of(j) + core
        return remote(own.at[c], own.at[c], own_send.at[j], own_recv.at[c], (s, target))

    def when_list(d, act):
        @pl.when(distant[d])
        def _():
            for q in range(2):
                act(far_copy(d, q))

            @pl.when((ends if d == 1 else 1 - front) == 1)
            def _():
                there = jnp.where(chip == 3, 1, 2) if d == 1 else 3 - chip
                act(side_copy(d, 2 * there + core))

        used = works_upper(s - 1 + 2 * d) == 1 - d

        @pl.when(near[d] & used)
        def _():
            act(list_copy(d, True))
            act(side_copy(d, c))

        @pl.when(near[d] & jnp.logical_not(used))
        def _():
            act(list_copy(d, False))

    for d in (1, 0):
        when_list(d, lambda copy: copy.start())
    for j in (1, 2, 3, 0):
        own_copy(j).start()

    def landed(buf, sem, i):
        return remote(buf.at[i], buf.at[i], sem.at[i], sem.at[i], (s, sib))

    def forward(buf, fwd, recv, i, k):
        return remote(buf.at[i], buf.at[i], fwd.at[k], recv.at[i], (s, sib))

    def same_plane():
        return remote(halo.at[c], halo.at[c], z_send.at[0], halo_recv.at[c], (s, beside))

    def other_plane(q):
        return remote(
            passing,
            halo.at[c],
            z_send.at[1 + q],
            halo_recv.at[c],
            (s, 2 * jnp.where(begins, jnp.where(ends == 1, 1 + q, 3 * q), 2 * front + q) + core),
        )

    def when_pass(d, act):
        @pl.when(near[d] & (upper == d))
        def _():
            act(same_plane())

        @pl.when(near[d] & (upper != d))
        def _():
            for q in range(2):
                act(other_plane(q))

    def pass_near():
        for d in range(2):

            @pl.when(near[d] & (upper == d))
            def _():
                landed(halo, halo_recv, c).wait_recv()
                same_plane().start()
                forward(halo, halo_fwd, halo_recv, c, 0).start()

            @pl.when(near[d] & (upper != d))
            def _():
                remote(passing, passing, pass_recv.at[0], pass_recv.at[0], (s, sib)).wait_recv()
                for q in range(2):
                    other_plane(q).start()

    for load in loads[6:]:
        load.wait()
    small[...] = jnp.zeros_like(small)
    small[0:6, 0:80] = geom_t[...].astype(F32)
    small[6:7, 0:80] = bias_one[...]
    small[7:8, 0:80] = bias_two[...]
    lane = iota((96, 128), 1)
    spread = jnp.where(
        (lane // ROWS * 12 + lane % ROWS == iota((96, 128), 0)) & (lane % ROWS < 12), 1.0, 0.0
    )
    small[8:16, :] = jnp.dot(
        jnp.broadcast_to(bias_three[...], (8, 96)),
        spread,
        preferred_element_type=F32,
        precision=lax.Precision.HIGHEST,
    )
    cols = jnp.transpose(small[...])
    spread = spread.astype(BF16)
    w_pre[:, 0:128] = jnp.dot(feat_weight[...], spread, preferred_element_type=F32).astype(BF16)
    lane16 = iota((80, 16), 1)
    w_side = jnp.zeros((80, 16), F32)
    for i in range(3):
        w_side = jnp.where(lane16 == i, cols[0:80, 3 + i : 4 + i], w_side)
    w_pre[:, 128:144] = w_side.astype(BF16)
    small[0:80, :] = jnp.dot(out_t[...], spread, preferred_element_type=F32)
    w_out[...] = jnp.transpose(small[...])[:, 0:80].astype(BF16)
    along_y = ((rank % GY).astype(F32) + 0.5) / GY
    along_z = ((2 * s + upper).astype(F32) + 0.5) / (ZD * slabs)
    wide[0:80, :] = jnp.broadcast_to(cols[0:80, 7:8], (80, 128))
    wide[80:208, :] = jnp.broadcast_to(cols[:, 8:9], (128, 128))
    slope = jnp.broadcast_to(cols[0:80, 0:1], (80, 128))
    base = jnp.broadcast_to(
        cols[0:80, 1:2] * along_y + cols[0:80, 2:3] * along_z + cols[0:80, 6:7], (80, 128)
    )
    for n in range(16):
        node[:, n * 128 : (n + 1) * 128] = base + slope * ((n + 0.5) / GX)

    @pl.when(jnp.logical_not(early))
    def _():
        lax.fori_loop(0, steps // 2, build, 0)

    pass_near()

    @pl.when(jnp.logical_not(early))
    def _():
        lax.fori_loop(steps // 2, steps, build, 0)

    extra = jnp.concatenate(
        [coords[...].astype(F32), jnp.ones((1, points), F32), jnp.zeros((12, points), F32)], axis=0
    )
    table[128:144, 0:points] = extra.astype(BF16)

    for j in range(1, 4):
        i = 2 * ((chip + j) % 4) + core
        landed(own, own_recv, i).wait_recv()
        forward(own, own_fwd, own_recv, i, j - 1).start()

    @pl.when(plane_near)
    def _():
        for q in range(1, 4):
            i = 2 * ((chip + q) % 4) + core
            landed(halo, halo_recv, i).wait_recv()
            forward(halo, halo_fwd, halo_recv, i, q).start()

    for j in range(4):
        landed(own, own_recv, 2 * ((chip + j) % 4) + 1 - core).wait_recv()

    table[0:128, 0:body] = own[:, :, 0:body].reshape(128, body)
    for i in range(8):
        rest = own[i].astype(F32)[12:16, :]
        rest = jnp.concatenate(
            [rest[:, g * tail : (g + 1) * tail] for g in range(3)] + [jnp.zeros((4, tail), F32)], axis=0
        )
        table[i * ROWS : (i + 1) * ROWS, body:points] = rest.astype(BF16)
    grid[...] = jnp.dot(table[:, 0:points], hot[0:points, :], preferred_element_type=F32)

    @pl.when(plane_far)
    def _():
        for q in range(4):
            i = 2 * (3 - q) + core
            landed(halo, halo_recv, i).wait_recv()
            forward(halo, halo_fwd, halo_recv, i, q).start()

    @pl.when(has_halo)
    def _():
        side_copy(0, c).wait_recv()
        for q in range(4):
            landed(halo, halo_recv, 2 * q + 1 - core).wait_recv()

    @pl.when(jnp.logical_not(has_halo))
    def _():
        halo[...] = jnp.zeros_like(halo)
        side_in[...] = jnp.zeros_like(side_in)

    table[0:128, points : points + hbody] = halo[...].reshape(128, hbody)
    for i in range(8):
        rest = halo[i].astype(F32)[12:16, :]
        rest = jnp.concatenate(
            [rest[:, g * htail : (g + 1) * htail] for g in range(3)] + [jnp.zeros((4, htail), F32)],
            axis=0,
        )
        table[i * ROWS : (i + 1) * ROWS, points + hbody : points + send] = rest.astype(BF16)
    rest = side_in[...].astype(F32)
    rest = jnp.concatenate([rest[4 * j : 4 * j + 4, :] for j in range(4)], axis=1)
    rest = jnp.concatenate([rest, jnp.zeros((12, send), F32)], axis=0)
    table[128:144, points : points + send] = rest.astype(BF16)

    values = grid[...] + jnp.dot(
        table[:, points : points + send],
        hot[points : points + send, :],
        preferred_element_type=F32,
    )
    pre = jnp.dot(w_pre[...], values.astype(BF16), preferred_element_type=F32)
    h1 = gelu(pre.astype(BF16).astype(F32) + node[...]).astype(BF16)
    h2 = jnp.dot(hidden_weight[...], h1, preferred_element_type=F32)
    h2 = gelu(h2 + jnp.concatenate([wide[0:80, :]] * 16, axis=1)).astype(BF16)
    kappa = jnp.dot(w_out[...], h2, preferred_element_type=F32)
    kappa = kappa + jnp.concatenate([wide[80:208, :]] * 16, axis=1)
    prod = kappa * values[0:128, :]

    lane8 = iota((8, 8, 128), 2)
    lane1 = iota((1, 128), 1)
    low_at = place * 16
    high_at = (place + 4) % 8 * 16
    acc = jnp.zeros((8, 8, 128), F32)
    number = jnp.ones((1, 128), F32)
    for n in range(16):
        at = slice(n * 128, (n + 1) * 128)
        total = jnp.sum(prod[:, at], axis=1, keepdims=True).reshape(8, ROWS, 1)
        acc = jnp.where(
            lane8 == low_at + n,
            total[:, 0:8],
            jnp.where(lane8 == high_at + n, total[:, 8:16], acc),
        )
        used = jnp.sum(values[128:136, at], axis=1, keepdims=True)[3:4]
        number = jnp.where((lane1 == low_at + n) | (lane1 == high_at + n), used, number)
    res[...] = acc / number[None]

    def res_copy(j):
        target = (c + j) % 8
        return remote(
            res.at[target], rcv.at[place], res_send.at[j - 1], res_recv.at[place], (s, target)
        )

    for j in range(1, 8):
        res_copy(j).start()
    rcv[place] = res[c]

    for j in range(4):
        own_copy(j).wait_send()
    for j in range(1, 4):
        forward(own, own_fwd, own_recv, c, j - 1).wait_send()
    for d in (1, 0):
        when_list(d, lambda copy: copy.wait_send())

    for d in range(2):
        when_pass(d, lambda copy: copy.wait_send())

    @pl.when(has_halo)
    def _():
        for q in range(4):
            forward(halo, halo_fwd, halo_recv, 2 * q + core, q).wait_send()

    for j in range(1, 8):
        landed(rcv, res_recv, (place + j) % 8).wait_recv()
    for j in range(1, 8):
        res_copy(j).wait_send()
    group = iota((8, 128), 1) // 16
    lower_rows = jnp.zeros((8, 128), F32)
    upper_rows = jnp.zeros((8, 128), F32)
    for i in range(8):
        lower_rows = jnp.where(group == i, rcv[i], lower_rows)
        upper_rows = jnp.where(group == (i + 4) % 8, rcv[i], upper_rows)
    out[0:8, :] = lower_rows
    out[8:12, :] = pltpu.roll(upper_rows, 64, 1)[0:4, :]


def shards(
    slabs,
    features,
    coords,
    send_rows,
    send_count,
    neighbours,
    neighbour_count,
    geom_weight,
    feat_weight,
    bias_one,
    hidden_weight,
    bias_two,
    out_weight,
    bias_three,
):
    points = features.shape[1]
    send = send_rows.shape[1]
    pairs = 16 * neighbours.shape[1]
    args = (
        features,
        coords,
        send_rows,
        send_count.reshape(2),
        neighbours,
        neighbour_count,
        geom_weight.T,
        feat_weight,
        bias_one.reshape(1, -1),
        hidden_weight,
        bias_two.reshape(1, -1),
        out_weight.T,
        bias_three.reshape(1, -1),
    )
    dma = pltpu.SemaphoreType.DMA
    held = [
        (pltpu.SMEM if i in (3, 5) else pltpu.VMEM)(a.shape, a.dtype) for i, a in enumerate(args)
    ]
    return pl.pallas_call(
        functools.partial(kernel, slabs),
        out_shape=jax.ShapeDtypeStruct((12, 128), F32),
        in_specs=[pl.BlockSpec(memory_space=pl.ANY)] * len(args),
        out_specs=pl.BlockSpec(memory_space=pltpu.VMEM),
        scratch_shapes=held
        + [
            pltpu.VMEM((8, ROWS, points * 3 // 4), BF16),
            pltpu.VMEM((8, ROWS, send * 3 // 4), BF16),
            pltpu.VMEM((2, ROWS, send * 3 // 4), BF16),
            pltpu.VMEM((ROWS, send * 3 // 4), BF16),
            pltpu.VMEM((2, ROWS, send // 4), BF16),
            pltpu.VMEM((ROWS, send // 4), BF16),
            pltpu.VMEM((9 * ROWS, points + send), BF16),
            pltpu.VMEM((points + send, pairs), BF16),
            pltpu.VMEM((9 * ROWS, pairs), F32),
            pltpu.VMEM((80, pairs), F32),
            pltpu.VMEM((ROWS, points), F32),
            pltpu.VMEM((ROWS, points * 3 // 4), F32),
            pltpu.VMEM((128, 128), F32),
            pltpu.VMEM((208, 128), F32),
            pltpu.VMEM((80, 9 * ROWS), BF16),
            pltpu.VMEM((128, 80), BF16),
            pltpu.VMEM((8, 8, 128), F32),
            pltpu.VMEM((8, 8, 128), F32),
            dma((len(args),)),
            dma((4,)),
            dma((8,)),
            dma((3,)),
            dma((2,)),
            dma((2,)),
            dma((8,)),
            dma((4,)),
            dma((1,)),
            dma((3,)),
            dma((2,)),
            dma((1,)),
            dma((7,)),
            dma((8,)),
        ],
        compiler_params=pltpu.CompilerParams(
            collective_id=0, has_side_effects=True, vmem_limit_bytes=60 * 2**20
        ),
    )(*args)


def solution(mesh):
    placed = (
        P("chan", "slab"),
        P(None, "slab"),
        P(None, "slab"),
        P(None, "slab"),
        P("slab", None),
        P("slab"),
        P(),
        P(),
        P(),
        P(),
        P(),
        P(),
        P(),
    )
    return jax.shard_map(
        functools.partial(shards, mesh.shape["slab"]),
        mesh=mesh,
        in_specs=placed,
        out_specs=P("chan", "slab"),
        check_vma=False,
    )
```

```python
import functools

import jax
import jax.numpy as jnp
from jax import lax
from jax.experimental import pallas as pl
from jax.experimental.pallas import tpu as pltpu
from jax.sharding import PartitionSpec as P

MESH = pl.DeviceIdType.MESH
ZD = 2
GX = 16
GY = 4
F32 = jnp.float32
BF16 = jnp.bfloat16
ROWS = 16
BLK = 256
C0 = 0.7978845608028654
C1 = 0.7978845608028654 * 0.044715


def gelu(x):
    half = 0.5 * x
    return half + half * jnp.tanh(x * (C0 + C1 * (x * x)))


def iota(shape, dim):
    return lax.broadcasted_iota(jnp.int32, shape, dim)


def one_hot(index, ramp):
    row = jnp.broadcast_to(index, (16, index.shape[1])).astype(BF16)
    full = jnp.concatenate([row] * (BLK // 16), axis=0)
    return jnp.where(ramp == full, jnp.ones_like(full), jnp.zeros_like(full))


def kernel(
    slabs,
    feat_h,
    coords_h,
    send_rows_h,
    send_count_h,
    nbr_h,
    counts_h,
    geom_h,
    feat_weight_h,
    bias_one_h,
    hidden_weight_h,
    bias_two_h,
    out_weight_h,
    bias_three_h,
    out,
    feat,
    coords,
    send_rows,
    send_count,
    nbr,
    counts,
    geom_t,
    feat_weight,
    bias_one,
    hidden_weight,
    bias_two,
    out_t,
    bias_three,
    own,
    halo,
    picked,
    passing,
    side_out,
    side_in,
    table,
    hot,
    grid,
    node,
    stage,
    pack,
    small,
    wide,
    w_pre,
    w_out,
    res,
    rcv,
    in_sem,
    own_send,
    own_recv,
    own_fwd,
    halo_send,
    far_send,
    halo_recv,
    halo_fwd,
    pass_recv,
    z_send,
    side_send,
    side_recv,
    res_send,
    res_recv,
):
    s = lax.axis_index("slab")
    c = lax.axis_index("chan")
    chip = c // 2
    core = c % 2
    sib = c + 1 - 2 * core
    front = 1 - chip // 2
    ends = 1 - (chip + 1) // 2 % 2
    half = s * 2 // slabs
    begins = s == slabs // 2

    def works_upper(slab):
        usual = jnp.where(slab * 2 // slabs == 0, front, 1 - front)
        return jnp.where(slab == slabs // 2, ends, usual)

    upper = works_upper(s)
    rank = 2 * jnp.where(begins, jnp.where(ends == 1, chip // 3, chip - 1), chip % 2) + core
    place = 4 * upper + rank
    early = (half == 0) & (front == 1)
    has_up = s < slabs - 1
    has_down = s > 0
    has = (has_down, has_up)
    has_halo = jnp.where(upper == 1, s < slabs - 1, s > 0)
    distant = (s == slabs // 2, s == slabs // 2 - 1)
    near = tuple(has[d] & jnp.logical_not(distant[d]) for d in range(2))
    plane_far = jnp.where(upper == 1, s == slabs // 2 - 1, s == slabs // 2)
    plane_near = has_halo & jnp.logical_not(plane_far)
    beside = 2 * jnp.where(begins, 3 - chip, chip + 1 - 2 * (chip % 2)) + core

    points = feat.shape[1]
    send = send_rows.shape[1]
    body = points * 3 // 4
    tail = points - body
    hbody = send * 3 // 4
    htail = send - hbody
    pairs = node.shape[1]

    barrier = pltpu.get_barrier_semaphore()
    for j in range(1, 8):
        pl.semaphore_signal(barrier, inc=1, device_id=(s, (c + j) % 8), device_id_type=MESH)

    for d in range(2):

        @pl.when(near[d])
        def _():
            pl.semaphore_signal(
                barrier, inc=1, device_id=(s - 1 + 2 * d, c), device_id_type=MESH
            )

        @pl.when(distant[d] & (upper == d))
        def _():
            for q in range(4):
                pl.semaphore_signal(
                    barrier,
                    inc=1,
                    device_id=(s - 1 + 2 * d, 2 * q + core),
                    device_id_type=MESH,
                )

    loads = [
        pltpu.make_async_copy(a, b, in_sem.at[i])
        for i, (a, b) in enumerate(
            [
                (feat_h, feat),
                (coords_h, coords),
                (send_rows_h, send_rows),
                (send_count_h, send_count),
                (nbr_h, nbr),
                (counts_h, counts),
                (geom_h, geom_t),
                (feat_weight_h, feat_weight),
                (bias_one_h, bias_one),
                (hidden_weight_h, hidden_weight),
                (bias_two_h, bias_two),
                (out_weight_h, out_t),
                (bias_three_h, bias_three),
            ]
        )
    ]
    for load in loads:
        load.start()
    for load in loads[:6]:
        load.wait()

    values = feat[...].astype(F32)
    pack[0:12, :] = values[:, 0:body]
    for g in range(3):
        pack[12:16, g * tail : (g + 1) * tail] = values[4 * g : 4 * g + 4, body:points]
    own[c] = pack[...].astype(BF16)

    stage[0:12, :] = values
    stage[12:15, :] = coords[...].astype(F32)
    stage[15:16, :] = jnp.ones((1, points), F32)
    slot = stage[...].astype(BF16)

    ramp = iota((BLK, 128), 0).astype(F32).astype(BF16)
    pieces = points // BLK
    stacked = jnp.concatenate([slot[:, h * BLK : (h + 1) * BLK] for h in range(pieces)], axis=0)
    for d in range(2):
        idx = send_rows[d : d + 1, :]
        idx = jnp.where(iota((1, send), 1) < send_count[d], idx, -1)
        low = (idx & (BLK - 1)).astype(F32)
        high = lax.shift_right_arithmetic(idx, 8)
        hots = jnp.concatenate(
            [one_hot(low[:, t * 128 : (t + 1) * 128], ramp) for t in range(send // 128)], axis=1
        )
        parts = jnp.dot(stacked, hots, preferred_element_type=F32)
        total = jnp.zeros((ROWS, send), F32)
        for h in range(pieces):
            total = total + jnp.where(high == h, parts[h * ROWS : (h + 1) * ROWS], 0.0)
        pack[0:12, 0:hbody] = total[0:12, 0:hbody]
        for g in range(3):
            pack[12:16, g * htail : (g + 1) * htail] = total[4 * g : 4 * g + 4, hbody:send]
        picked[d] = pack[:, 0:hbody].astype(BF16)
        for j in range(4):
            pack[4 * j : 4 * j + 4, 0:htail] = total[12:16, j * htail : (j + 1) * htail]
        side_out[d] = pack[:, 0:htail].astype(BF16)

    first = pl.multiple_of(place * 16, 16)
    idx = nbr[pl.ds(first, 16), :]
    idx = idx - jnp.where(idx >= points, send * upper, 0)
    slots = iota((1, 128), 1)
    rows = []
    for n in range(16):
        rows.append(jnp.where(slots < counts[first + n], idx[n : n + 1, :], -1))
    lows = [(r & (BLK - 1)).astype(F32) for r in rows]
    highs = [lax.shift_right_arithmetic(r, 8) for r in rows]

    def build(kb, carry):
        at = pl.ds(pl.multiple_of(kb * BLK, BLK), BLK)
        for n in range(16):
            pick = jnp.where(highs[n] == kb, lows[n], -1.0)
            hot[at, n * 128 : (n + 1) * 128] = one_hot(pick, ramp)
        return carry

    steps = (points + send) // BLK

    @pl.when(early)
    def _():
        lax.fori_loop(0, steps, build, 0)

    others = [jnp.where(has[d], jnp.where(distant[d], 2, 1), 0) for d in range(2)]
    pl.semaphore_wait(barrier, 7 + others[0] + others[1])

    def remote(src, dst, sem_out, sem_in, target):
        return pltpu.make_async_remote_copy(
            src_ref=src,
            dst_ref=dst,
            send_sem=sem_out,
            recv_sem=sem_in,
            device_id=target,
            device_id_type=MESH,
        )

    def list_copy(d, direct):
        return remote(
            picked.at[d],
            halo.at[c] if direct else passing,
            halo_send.at[d],
            halo_recv.at[c] if direct else pass_recv.at[0],
            (s - 1 + 2 * d, c),
        )

    def far_copy(d, q):
        return remote(
            picked.at[d],
            halo.at[c],
            far_send.at[q],
            halo_recv.at[c],
            (s - 1 + 2 * d, 2 * (q + d) + core),
        )

    def side_copy(d, target):
        return remote(
            side_out.at[d], side_in, side_send.at[d], side_recv.at[0], (s - 1 + 2 * d, target)
        )

    def there_of(j):
        up = j - 1 + jnp.where(chip <= j - 1, 1, 0)
        down = 4 - j - jnp.where(3 - chip <= j - 1, 1, 0)
        return jnp.where(chip < 2, down, up)

    def own_copy(j):
        target = sib if j == 0 else 2 * there_of(j) + core
        return remote(own.at[c], own.at[c], own_send.at[j], own_recv.at[c], (s, target))

    def when_list(d, act):
        @pl.when(distant[d])
        def _():
            for q in range(2):
                act(far_copy(d, q))

            @pl.when((ends if d == 1 else 1 - front) == 1)
            def _():
                there = jnp.where(chip == 3, 1, 2) if d == 1 else 3 - chip
                act(side_copy(d, 2 * there + core))

        used = works_upper(s - 1 + 2 * d) == 1 - d

        @pl.when(near[d] & used)
        def _():
            act(list_copy(d, True))
            act(side_copy(d, c))

        @pl.when(near[d] & jnp.logical_not(used))
        def _():
            act(list_copy(d, False))

    for d in (1, 0):
        when_list(d, lambda copy: copy.start())
    for j in (1, 2, 3, 0):
        own_copy(j).start()

    def landed(buf, sem, i):
        return remote(buf.at[i], buf.at[i], sem.at[i], sem.at[i], (s, sib))

    def forward(buf, fwd, recv, i, k):
        return remote(buf.at[i], buf.at[i], fwd.at[k], recv.at[i], (s, sib))

    def same_plane():
        return remote(halo.at[c], halo.at[c], z_send.at[0], halo_recv.at[c], (s, beside))

    def other_plane(q):
        return remote(
            passing,
            halo.at[c],
            z_send.at[1 + q],
            halo_recv.at[c],
            (s, 2 * jnp.where(begins, jnp.where(ends == 1, 1 + q, 3 * q), 2 * front + q) + core),
        )

    def when_pass(d, act):
        @pl.when(near[d] & (upper == d))
        def _():
            act(same_plane())

        @pl.when(near[d] & (upper != d))
        def _():
            for q in range(2):
                act(other_plane(q))

    def pass_near():
        for d in range(2):

            @pl.when(near[d] & (upper != d))
            def _():
                remote(passing, passing, pass_recv.at[0], pass_recv.at[0], (s, sib)).wait_recv()
                for q in range(2):
                    other_plane(q).start()

        for d in range(2):

            @pl.when(near[d] & (upper == d))
            def _():
                landed(halo, halo_recv, c).wait_recv()
                same_plane().start()
                forward(halo, halo_fwd, halo_recv, c, 0).start()

    for load in loads[6:]:
        load.wait()
    small[...] = jnp.zeros_like(small)
    small[0:6, 0:80] = geom_t[...].astype(F32)
    small[6:7, 0:80] = bias_one[...]
    small[7:8, 0:80] = bias_two[...]
    lane = iota((96, 128), 1)
    spread = jnp.where(
        (lane // ROWS * 12 + lane % ROWS == iota((96, 128), 0)) & (lane % ROWS < 12), 1.0, 0.0
    )
    small[8:16, :] = jnp.dot(
        jnp.broadcast_to(bias_three[...], (8, 96)),
        spread,
        preferred_element_type=F32,
        precision=lax.Precision.HIGHEST,
    )
    cols = jnp.transpose(small[...])
    spread = spread.astype(BF16)
    w_pre[:, 0:128] = jnp.dot(feat_weight[...], spread, preferred_element_type=F32).astype(BF16)
    lane16 = iota((80, 16), 1)
    w_side = jnp.zeros((80, 16), F32)
    for i in range(3):
        w_side = jnp.where(lane16 == i, cols[0:80, 3 + i : 4 + i], w_side)
    w_pre[:, 128:144] = w_side.astype(BF16)
    small[0:80, :] = jnp.dot(out_t[...], spread, preferred_element_type=F32)
    w_out[...] = jnp.transpose(small[...])[:, 0:80].astype(BF16)
    along_y = ((rank % GY).astype(F32) + 0.5) / GY
    along_z = ((2 * s + upper).astype(F32) + 0.5) / (ZD * slabs)
    wide[0:80, :] = jnp.broadcast_to(cols[0:80, 7:8], (80, 128))
    wide[80:208, :] = jnp.broadcast_to(cols[:, 8:9], (128, 128))
    slope = jnp.broadcast_to(cols[0:80, 0:1], (80, 128))
    base = jnp.broadcast_to(
        cols[0:80, 1:2] * along_y + cols[0:80, 2:3] * along_z + cols[0:80, 6:7], (80, 128)
    )
    for n in range(16):
        node[:, n * 128 : (n + 1) * 128] = base + slope * ((n + 0.5) / GX)

    @pl.when(jnp.logical_not(early))
    def _():
        lax.fori_loop(0, steps // 2, build, 0)

    pass_near()

    @pl.when(jnp.logical_not(early))
    def _():
        lax.fori_loop(steps // 2, steps, build, 0)

    extra = jnp.concatenate(
        [coords[...].astype(F32), jnp.ones((1, points), F32), jnp.zeros((12, points), F32)], axis=0
    )
    table[128:144, 0:points] = extra.astype(BF16)

    for j in range(1, 4):
        i = 2 * ((chip + j) % 4) + core
        landed(own, own_recv, i).wait_recv()
        forward(own, own_fwd, own_recv, i, j - 1).start()

    for j in range(4):
        landed(own, own_recv, 2 * ((chip + j) % 4) + 1 - core).wait_recv()

    table[0:128, 0:body] = own[:, :, 0:body].reshape(128, body)
    for i in range(8):
        rest = own[i].astype(F32)[12:16, :]
        rest = jnp.concatenate(
            [rest[:, g * tail : (g + 1) * tail] for g in range(3)] + [jnp.zeros((4, tail), F32)], axis=0
        )
        table[i * ROWS : (i + 1) * ROWS, body:points] = rest.astype(BF16)
    cut = pairs * 4 // 8

    def gather_own(low, high):
        grid[:, low:high] = jnp.dot(
            table[:, 0:points], hot[0:points, low:high], preferred_element_type=F32
        )

    gather_own(0, cut)

    @pl.when(plane_near)
    def _():
        for q in range(1, 4):
            i = 2 * ((chip + q) % 4) + core
            landed(halo, halo_recv, i).wait_recv()
            forward(halo, halo_fwd, halo_recv, i, q).start()

    gather_own(cut, pairs)

    @pl.when(plane_far)
    def _():
        for q in range(4):
            i = 2 * (3 - q) + core
            landed(halo, halo_recv, i).wait_recv()
            forward(halo, halo_fwd, halo_recv, i, q).start()

    @pl.when(has_halo)
    def _():
        side_copy(0, c).wait_recv()
        for q in range(4):
            landed(halo, halo_recv, 2 * q + 1 - core).wait_recv()

    @pl.when(jnp.logical_not(has_halo))
    def _():
        halo[...] = jnp.zeros_like(halo)
        side_in[...] = jnp.zeros_like(side_in)

    table[0:128, points : points + hbody] = halo[...].reshape(128, hbody)
    for i in range(8):
        rest = halo[i].astype(F32)[12:16, :]
        rest = jnp.concatenate(
            [rest[:, g * htail : (g + 1) * htail] for g in range(3)] + [jnp.zeros((4, htail), F32)],
            axis=0,
        )
        table[i * ROWS : (i + 1) * ROWS, points + hbody : points + send] = rest.astype(BF16)
    rest = side_in[...].astype(F32)
    rest = jnp.concatenate([rest[4 * j : 4 * j + 4, :] for j in range(4)], axis=1)
    rest = jnp.concatenate([rest, jnp.zeros((12, send), F32)], axis=0)
    table[128:144, points : points + send] = rest.astype(BF16)

    values = grid[...] + jnp.dot(
        table[:, points : points + send],
        hot[points : points + send, :],
        preferred_element_type=F32,
    )
    pre = jnp.dot(w_pre[...], values.astype(BF16), preferred_element_type=F32)
    h1 = gelu(pre.astype(BF16).astype(F32) + node[...]).astype(BF16)
    h2 = jnp.dot(hidden_weight[...], h1, preferred_element_type=F32)
    h2 = gelu(h2 + jnp.concatenate([wide[0:80, :]] * 16, axis=1)).astype(BF16)
    kappa = jnp.dot(w_out[...], h2, preferred_element_type=F32)
    kappa = kappa + jnp.concatenate([wide[80:208, :]] * 16, axis=1)
    prod = kappa * values[0:128, :]

    lane8 = iota((8, 8, 128), 2)
    lane1 = iota((1, 128), 1)
    low_at = place * 16
    high_at = (place + 4) % 8 * 16
    acc = jnp.zeros((8, 8, 128), F32)
    number = jnp.ones((1, 128), F32)
    for n in range(16):
        at = slice(n * 128, (n + 1) * 128)
        total = jnp.sum(prod[:, at], axis=1, keepdims=True).reshape(8, ROWS, 1)
        acc = jnp.where(
            lane8 == low_at + n,
            total[:, 0:8],
            jnp.where(lane8 == high_at + n, total[:, 8:16], acc),
        )
        used = jnp.sum(values[128:136, at], axis=1, keepdims=True)[3:4]
        number = jnp.where((lane1 == low_at + n) | (lane1 == high_at + n), used, number)
    res[...] = acc / number[None]

    def res_copy(j):
        target = (c + j) % 8
        return remote(
            res.at[target], rcv.at[place], res_send.at[j - 1], res_recv.at[place], (s, target)
        )

    for j in range(1, 8):
        res_copy(j).start()
    rcv[place] = res[c]

    for j in range(4):
        own_copy(j).wait_send()
    for j in range(1, 4):
        forward(own, own_fwd, own_recv, c, j - 1).wait_send()
    for d in (1, 0):
        when_list(d, lambda copy: copy.wait_send())

    for d in range(2):
        when_pass(d, lambda copy: copy.wait_send())

    @pl.when(has_halo)
    def _():
        for q in range(4):
            forward(halo, halo_fwd, halo_recv, 2 * q + core, q).wait_send()

    for j in range(1, 8):
        landed(rcv, res_recv, (place + j) % 8).wait_recv()
    for j in range(1, 8):
        res_copy(j).wait_send()
    group = iota((8, 128), 1) // 16
    lower_rows = jnp.zeros((8, 128), F32)
    upper_rows = jnp.zeros((8, 128), F32)
    for i in range(8):
        lower_rows = jnp.where(group == i, rcv[i], lower_rows)
        upper_rows = jnp.where(group == (i + 4) % 8, rcv[i], upper_rows)
    out[0:8, :] = lower_rows
    out[8:12, :] = pltpu.roll(upper_rows, 64, 1)[0:4, :]


def shards(
    slabs,
    features,
    coords,
    send_rows,
    send_count,
    neighbours,
    neighbour_count,
    geom_weight,
    feat_weight,
    bias_one,
    hidden_weight,
    bias_two,
    out_weight,
    bias_three,
):
    points = features.shape[1]
    send = send_rows.shape[1]
    pairs = 16 * neighbours.shape[1]
    args = (
        features,
        coords,
        send_rows,
        send_count.reshape(2),
        neighbours,
        neighbour_count,
        geom_weight.T,
        feat_weight,
        bias_one.reshape(1, -1),
        hidden_weight,
        bias_two.reshape(1, -1),
        out_weight.T,
        bias_three.reshape(1, -1),
    )
    dma = pltpu.SemaphoreType.DMA
    held = [
        (pltpu.SMEM if i in (3, 5) else pltpu.VMEM)(a.shape, a.dtype) for i, a in enumerate(args)
    ]
    return pl.pallas_call(
        functools.partial(kernel, slabs),
        out_shape=jax.ShapeDtypeStruct((12, 128), F32),
        in_specs=[pl.BlockSpec(memory_space=pl.ANY)] * len(args),
        out_specs=pl.BlockSpec(memory_space=pltpu.VMEM),
        scratch_shapes=held
        + [
            pltpu.VMEM((8, ROWS, points * 3 // 4), BF16),
            pltpu.VMEM((8, ROWS, send * 3 // 4), BF16),
            pltpu.VMEM((2, ROWS, send * 3 // 4), BF16),
            pltpu.VMEM((ROWS, send * 3 // 4), BF16),
            pltpu.VMEM((2, ROWS, send // 4), BF16),
            pltpu.VMEM((ROWS, send // 4), BF16),
            pltpu.VMEM((9 * ROWS, points + send), BF16),
            pltpu.VMEM((points + send, pairs), BF16),
            pltpu.VMEM((9 * ROWS, pairs), F32),
            pltpu.VMEM((80, pairs), F32),
            pltpu.VMEM((ROWS, points), F32),
            pltpu.VMEM((ROWS, points * 3 // 4), F32),
            pltpu.VMEM((128, 128), F32),
            pltpu.VMEM((208, 128), F32),
            pltpu.VMEM((80, 9 * ROWS), BF16),
            pltpu.VMEM((128, 80), BF16),
            pltpu.VMEM((8, 8, 128), F32),
            pltpu.VMEM((8, 8, 128), F32),
            dma((len(args),)),
            dma((4,)),
            dma((8,)),
            dma((3,)),
            dma((2,)),
            dma((2,)),
            dma((8,)),
            dma((4,)),
            dma((1,)),
            dma((3,)),
            dma((2,)),
            dma((1,)),
            dma((7,)),
            dma((8,)),
        ],
        compiler_params=pltpu.CompilerParams(
            collective_id=0, has_side_effects=True, vmem_limit_bytes=60 * 2**20
        ),
    )(*args)


def solution(mesh):
    placed = (
        P("chan", "slab"),
        P(None, "slab"),
        P(None, "slab"),
        P(None, "slab"),
        P("slab", None),
        P("slab"),
        P(),
        P(),
        P(),
        P(),
        P(),
        P(),
        P(),
    )
    return jax.shard_map(
        functools.partial(shards, mesh.shape["slab"]),
        mesh=mesh,
        in_specs=placed,
        out_specs=P("chan", "slab"),
        check_vma=False,
    )
```

```python
import functools

import jax
import jax.numpy as jnp
from jax import lax
from jax.experimental import pallas as pl
from jax.experimental.pallas import tpu as pltpu
from jax.sharding import PartitionSpec as P

MESH = pl.DeviceIdType.MESH
ZD = 2
GX = 16
GY = 4
F32 = jnp.float32
BF16 = jnp.bfloat16
ROWS = 16
BLK = 256
C0 = 0.7978845608028654
C1 = 0.7978845608028654 * 0.044715


def gelu(x):
    half = 0.5 * x
    return half + half * jnp.tanh(x * (C0 + C1 * (x * x)))


def iota(shape, dim):
    return lax.broadcasted_iota(jnp.int32, shape, dim)


def one_hot(index, ramp):
    row = jnp.broadcast_to(index, (16, index.shape[1])).astype(BF16)
    full = jnp.concatenate([row] * (BLK // 16), axis=0)
    return jnp.where(ramp == full, jnp.ones_like(full), jnp.zeros_like(full))


def kernel(
    slabs,
    feat_h,
    coords_h,
    send_rows_h,
    send_count_h,
    nbr_h,
    counts_h,
    geom_h,
    feat_weight_h,
    bias_one_h,
    hidden_weight_h,
    bias_two_h,
    out_weight_h,
    bias_three_h,
    out,
    feat,
    coords,
    send_rows,
    send_count,
    nbr,
    counts,
    geom_t,
    feat_weight,
    bias_one,
    hidden_weight,
    bias_two,
    out_t,
    bias_three,
    own,
    halo,
    picked,
    passing,
    side_out,
    side_in,
    table,
    hot,
    grid,
    node,
    stage,
    pack,
    small,
    wide,
    w_pre,
    w_out,
    res,
    rcv,
    in_sem,
    own_send,
    own_recv,
    own_fwd,
    halo_send,
    far_send,
    halo_recv,
    halo_fwd,
    pass_recv,
    z_send,
    side_send,
    side_recv,
    res_send,
    res_recv,
):
    s = lax.axis_index("slab")
    c = lax.axis_index("chan")
    chip = c // 2
    core = c % 2
    sib = c + 1 - 2 * core
    front = 1 - chip // 2
    ends = 1 - (chip + 1) // 2 % 2
    half = s * 2 // slabs
    begins = s == slabs // 2

    def works_upper(slab):
        usual = jnp.where(slab * 2 // slabs == 0, front, 1 - front)
        return jnp.where(slab == slabs // 2, ends, usual)

    upper = works_upper(s)
    rank = 2 * jnp.where(begins, jnp.where(ends == 1, chip // 3, chip - 1), chip % 2) + core
    place = 4 * upper + rank
    early = (half == 0) & (front == 1)
    has_up = s < slabs - 1
    has_down = s > 0
    has = (has_down, has_up)
    has_halo = jnp.where(upper == 1, s < slabs - 1, s > 0)
    distant = (s == slabs // 2, s == slabs // 2 - 1)
    near = tuple(has[d] & jnp.logical_not(distant[d]) for d in range(2))
    plane_far = jnp.where(upper == 1, s == slabs // 2 - 1, s == slabs // 2)
    plane_near = has_halo & jnp.logical_not(plane_far)
    beside = 2 * jnp.where(begins, 3 - chip, chip + 1 - 2 * (chip % 2)) + core

    points = feat.shape[1]
    send = send_rows.shape[1]
    body = points * 3 // 4
    tail = points - body
    hbody = send * 3 // 4
    htail = send - hbody
    pairs = node.shape[1]

    barrier = pltpu.get_barrier_semaphore()
    for j in range(1, 8):
        pl.semaphore_signal(barrier, inc=1, device_id=(s, (c + j) % 8), device_id_type=MESH)

    for d in range(2):

        @pl.when(near[d])
        def _():
            pl.semaphore_signal(
                barrier, inc=1, device_id=(s - 1 + 2 * d, c), device_id_type=MESH
            )

        @pl.when(distant[d] & (upper == d))
        def _():
            for q in range(4):
                pl.semaphore_signal(
                    barrier,
                    inc=1,
                    device_id=(s - 1 + 2 * d, 2 * q + core),
                    device_id_type=MESH,
                )

    loads = [
        pltpu.make_async_copy(a, b, in_sem.at[i])
        for i, (a, b) in enumerate(
            [
                (feat_h, feat),
                (coords_h, coords),
                (send_rows_h, send_rows),
                (send_count_h, send_count),
                (nbr_h, nbr),
                (counts_h, counts),
                (geom_h, geom_t),
                (feat_weight_h, feat_weight),
                (bias_one_h, bias_one),
                (hidden_weight_h, hidden_weight),
                (bias_two_h, bias_two),
                (out_weight_h, out_t),
                (bias_three_h, bias_three),
            ]
        )
    ]
    for load in loads:
        load.start()
    for load in loads[:6]:
        load.wait()

    values = feat[...].astype(F32)
    pack[0:12, :] = values[:, 0:body]
    for g in range(3):
        pack[12:16, g * tail : (g + 1) * tail] = values[4 * g : 4 * g + 4, body:points]
    own[c] = pack[...].astype(BF16)

    stage[0:12, :] = values
    stage[12:15, :] = coords[...].astype(F32)
    stage[15:16, :] = jnp.ones((1, points), F32)
    slot = stage[...].astype(BF16)

    ramp = iota((BLK, 128), 0).astype(F32).astype(BF16)
    pieces = points // BLK
    stacked = jnp.concatenate([slot[:, h * BLK : (h + 1) * BLK] for h in range(pieces)], axis=0)
    for d in range(2):
        idx = send_rows[d : d + 1, :]
        idx = jnp.where(iota((1, send), 1) < send_count[d], idx, -1)
        low = (idx & (BLK - 1)).astype(F32)
        high = lax.shift_right_arithmetic(idx, 8)
        hots = jnp.concatenate(
            [one_hot(low[:, t * 128 : (t + 1) * 128], ramp) for t in range(send // 128)], axis=1
        )
        parts = jnp.dot(stacked, hots, preferred_element_type=F32)
        total = jnp.zeros((ROWS, send), F32)
        for h in range(pieces):
            total = total + jnp.where(high == h, parts[h * ROWS : (h + 1) * ROWS], 0.0)
        pack[0:12, 0:hbody] = total[0:12, 0:hbody]
        for g in range(3):
            pack[12:16, g * htail : (g + 1) * htail] = total[4 * g : 4 * g + 4, hbody:send]
        picked[d] = pack[:, 0:hbody].astype(BF16)
        for j in range(4):
            pack[4 * j : 4 * j + 4, 0:htail] = total[12:16, j * htail : (j + 1) * htail]
        side_out[d] = pack[:, 0:htail].astype(BF16)

    first = pl.multiple_of(place * 16, 16)
    idx = nbr[pl.ds(first, 16), :]
    idx = idx - jnp.where(idx >= points, send * upper, 0)
    slots = iota((1, 128), 1)
    rows = []
    for n in range(16):
        rows.append(jnp.where(slots < counts[first + n], idx[n : n + 1, :], -1))
    lows = [(r & (BLK - 1)).astype(F32) for r in rows]
    highs = [lax.shift_right_arithmetic(r, 8) for r in rows]

    def build(kb, carry):
        at = pl.ds(pl.multiple_of(kb * BLK, BLK), BLK)
        for n in range(16):
            pick = jnp.where(highs[n] == kb, lows[n], -1.0)
            hot[at, n * 128 : (n + 1) * 128] = one_hot(pick, ramp)
        return carry

    steps = (points + send) // BLK

    @pl.when(early)
    def _():
        lax.fori_loop(0, steps, build, 0)

    others = [jnp.where(has[d], jnp.where(distant[d], 2, 1), 0) for d in range(2)]
    pl.semaphore_wait(barrier, 7 + others[0] + others[1])

    def remote(src, dst, sem_out, sem_in, target):
        return pltpu.make_async_remote_copy(
            src_ref=src,
            dst_ref=dst,
            send_sem=sem_out,
            recv_sem=sem_in,
            device_id=target,
            device_id_type=MESH,
        )

    def list_copy(d, direct):
        return remote(
            picked.at[d],
            halo.at[c] if direct else passing,
            halo_send.at[d],
            halo_recv.at[c] if direct else pass_recv.at[0],
            (s - 1 + 2 * d, c),
        )

    def far_copy(d, q):
        return remote(
            picked.at[d],
            halo.at[c],
            far_send.at[q],
            halo_recv.at[c],
            (s - 1 + 2 * d, 2 * (q + d) + core),
        )

    def side_copy(d, target):
        return remote(
            side_out.at[d], side_in, side_send.at[d], side_recv.at[0], (s - 1 + 2 * d, target)
        )

    def there_of(j):
        up = j - 1 + jnp.where(chip <= j - 1, 1, 0)
        down = 4 - j - jnp.where(3 - chip <= j - 1, 1, 0)
        return jnp.where(chip < 2, down, up)

    def own_copy(j):
        target = sib if j == 0 else 2 * there_of(j) + core
        return remote(own.at[c], own.at[c], own_send.at[j], own_recv.at[c], (s, target))

    def when_list(d, act):
        @pl.when(distant[d])
        def _():
            for q in range(2):
                act(far_copy(d, q))

            @pl.when((ends if d == 1 else 1 - front) == 1)
            def _():
                there = jnp.where(chip == 3, 1, 2) if d == 1 else 3 - chip
                act(side_copy(d, 2 * there + core))

        used = works_upper(s - 1 + 2 * d) == 1 - d

        @pl.when(near[d] & used)
        def _():
            act(list_copy(d, True))
            act(side_copy(d, c))

        @pl.when(near[d] & jnp.logical_not(used))
        def _():
            act(list_copy(d, False))

    for d in (1, 0):
        when_list(d, lambda copy: copy.start())
    for j in (1, 2, 3, 0):
        own_copy(j).start()

    def landed(buf, sem, i):
        return remote(buf.at[i], buf.at[i], sem.at[i], sem.at[i], (s, sib))

    def forward(buf, fwd, recv, i, k):
        return remote(buf.at[i], buf.at[i], fwd.at[k], recv.at[i], (s, sib))

    def same_plane():
        return remote(halo.at[c], halo.at[c], z_send.at[0], halo_recv.at[c], (s, beside))

    def other_plane(q):
        return remote(
            passing,
            halo.at[c],
            z_send.at[1 + q],
            halo_recv.at[c],
            (s, 2 * jnp.where(begins, jnp.where(ends == 1, 1 + q, 3 * q), 2 * front + q) + core),
        )

    def when_pass(d, act):
        @pl.when(near[d] & (upper == d))
        def _():
            act(same_plane())

        @pl.when(near[d] & (upper != d))
        def _():
            for q in range(2):
                act(other_plane(q))

    def pass_near():
        for d in range(2):

            @pl.when(near[d] & (upper != d))
            def _():
                remote(passing, passing, pass_recv.at[0], pass_recv.at[0], (s, sib)).wait_recv()
                for q in range(2):
                    other_plane(q).start()

        for d in range(2):

            @pl.when(near[d] & (upper == d))
            def _():
                landed(halo, halo_recv, c).wait_recv()
                same_plane().start()
                forward(halo, halo_fwd, halo_recv, c, 0).start()

    for load in loads[6:]:
        load.wait()
    small[...] = jnp.zeros_like(small)
    small[0:6, 0:80] = geom_t[...].astype(F32)
    small[6:7, 0:80] = bias_one[...]
    small[7:8, 0:80] = bias_two[...]
    lane = iota((96, 128), 1)
    spread = jnp.where(
        (lane // ROWS * 12 + lane % ROWS == iota((96, 128), 0)) & (lane % ROWS < 12), 1.0, 0.0
    )
    small[8:16, :] = jnp.dot(
        jnp.broadcast_to(bias_three[...], (8, 96)),
        spread,
        preferred_element_type=F32,
        precision=lax.Precision.HIGHEST,
    )
    cols = jnp.transpose(small[...])
    spread = spread.astype(BF16)
    w_pre[:, 0:128] = jnp.dot(feat_weight[...], spread, preferred_element_type=F32).astype(BF16)
    lane16 = iota((80, 16), 1)
    w_side = jnp.zeros((80, 16), F32)
    for i in range(3):
        w_side = jnp.where(lane16 == i, cols[0:80, 3 + i : 4 + i], w_side)
    w_pre[:, 128:144] = w_side.astype(BF16)
    small[0:80, :] = jnp.dot(out_t[...], spread, preferred_element_type=F32)
    w_out[...] = jnp.transpose(small[...])[:, 0:80].astype(BF16)
    along_y = ((rank % GY).astype(F32) + 0.5) / GY
    along_z = ((2 * s + upper).astype(F32) + 0.5) / (ZD * slabs)
    wide[0:80, :] = jnp.broadcast_to(cols[0:80, 7:8], (80, 128))
    wide[80:208, :] = jnp.broadcast_to(cols[:, 8:9], (128, 128))
    slope = jnp.broadcast_to(cols[0:80, 0:1], (80, 128))
    base = jnp.broadcast_to(
        cols[0:80, 1:2] * along_y + cols[0:80, 2:3] * along_z + cols[0:80, 6:7], (80, 128)
    )
    for n in range(16):
        node[:, n * 128 : (n + 1) * 128] = base + slope * ((n + 0.5) / GX)

    @pl.when(jnp.logical_not(early))
    def _():
        lax.fori_loop(0, steps // 2, build, 0)

    pass_near()

    @pl.when(jnp.logical_not(early))
    def _():
        lax.fori_loop(steps // 2, steps, build, 0)

    extra = jnp.concatenate(
        [coords[...].astype(F32), jnp.ones((1, points), F32), jnp.zeros((12, points), F32)], axis=0
    )
    table[128:144, 0:points] = extra.astype(BF16)

    for j in range(1, 4):
        i = 2 * ((chip + j) % 4) + core
        landed(own, own_recv, i).wait_recv()
        forward(own, own_fwd, own_recv, i, j - 1).start()

    for j in range(4):
        landed(own, own_recv, 2 * ((chip + j) % 4) + 1 - core).wait_recv()

    table[0:128, 0:body] = own[:, :, 0:body].reshape(128, body)
    for i in range(8):
        rest = own[i].astype(F32)[12:16, :]
        rest = jnp.concatenate(
            [rest[:, g * tail : (g + 1) * tail] for g in range(3)] + [jnp.zeros((4, tail), F32)], axis=0
        )
        table[i * ROWS : (i + 1) * ROWS, body:points] = rest.astype(BF16)
    cut = pairs * 4 // 8

    def gather_own(low, high):
        grid[:, low:high] = jnp.dot(
            table[:, 0:points], hot[0:points, low:high], preferred_element_type=F32
        )

    gather_own(0, cut)

    @pl.when(plane_near)
    def _():
        for q in range(1, 4):
            i = 2 * ((chip + q) % 4) + core
            landed(halo, halo_recv, i).wait_recv()
            forward(halo, halo_fwd, halo_recv, i, q).start()

    gather_own(cut, pairs)

    @pl.when(plane_far)
    def _():
        for q in range(4):
            i = 2 * (3 - q) + core
            landed(halo, halo_recv, i).wait_recv()
            forward(halo, halo_fwd, halo_recv, i, q).start()

    @pl.when(has_halo)
    def _():
        side_copy(0, c).wait_recv()
        for q in range(4):
            landed(halo, halo_recv, 2 * q + 1 - core).wait_recv()

    @pl.when(jnp.logical_not(has_halo))
    def _():
        halo[...] = jnp.zeros_like(halo)
        side_in[...] = jnp.zeros_like(side_in)

    table[0:128, points : points + hbody] = halo[...].reshape(128, hbody)
    for i in range(8):
        rest = halo[i].astype(F32)[12:16, :]
        rest = jnp.concatenate(
            [rest[:, g * htail : (g + 1) * htail] for g in range(3)] + [jnp.zeros((4, htail), F32)],
            axis=0,
        )
        table[i * ROWS : (i + 1) * ROWS, points + hbody : points + send] = rest.astype(BF16)
    rest = side_in[...].astype(F32)
    rest = jnp.concatenate([rest[4 * j : 4 * j + 4, :] for j in range(4)], axis=1)
    rest = jnp.concatenate([rest, jnp.zeros((12, send), F32)], axis=0)
    table[128:144, points : points + send] = rest.astype(BF16)

    values = grid[...] + jnp.dot(
        table[:, points : points + send],
        hot[points : points + send, :],
        preferred_element_type=F32,
    )
    pre = jnp.dot(w_pre[...], values.astype(BF16), preferred_element_type=F32)
    h1 = gelu(pre.astype(BF16).astype(F32) + node[...]).astype(BF16)
    h2 = jnp.dot(hidden_weight[...], h1, preferred_element_type=F32)
    h2 = gelu(h2 + jnp.concatenate([wide[0:80, :]] * 16, axis=1)).astype(BF16)
    kappa = jnp.dot(w_out[...], h2, preferred_element_type=F32)
    kappa = kappa + jnp.concatenate([wide[80:208, :]] * 16, axis=1)
    prod = kappa * values[0:128, :]

    lane8 = iota((8, 8, 128), 2)
    lane1 = iota((1, 128), 1)
    low_at = place * 16
    high_at = (place + 4) % 8 * 16
    acc = jnp.zeros((8, 8, 128), F32)
    number = jnp.ones((1, 128), F32)
    for n in range(16):
        at = slice(n * 128, (n + 1) * 128)
        total = jnp.sum(prod[:, at], axis=1, keepdims=True).reshape(8, ROWS, 1)
        acc = jnp.where(
            lane8 == low_at + n,
            total[:, 0:8],
            jnp.where(lane8 == high_at + n, total[:, 8:16], acc),
        )
        used = jnp.sum(values[128:136, at], axis=1, keepdims=True)[3:4]
        number = jnp.where((lane1 == low_at + n) | (lane1 == high_at + n), used, number)
    res[...] = acc / number[None]

    def res_copy(j):
        target = (c + j) % 8
        return remote(
            res.at[target], rcv.at[place], res_send.at[j - 1], res_recv.at[place], (s, target)
        )

    for j in range(1, 8):
        res_copy(j).start()
    rcv[place] = res[c]

    for j in range(4):
        own_copy(j).wait_send()
    for j in range(1, 4):
        forward(own, own_fwd, own_recv, c, j - 1).wait_send()
    for d in (1, 0):
        when_list(d, lambda copy: copy.wait_send())

    for d in range(2):
        when_pass(d, lambda copy: copy.wait_send())

    @pl.when(has_halo)
    def _():
        for q in range(4):
            forward(halo, halo_fwd, halo_recv, 2 * q + core, q).wait_send()

    for j in range(1, 8):
        landed(rcv, res_recv, (place + j) % 8).wait_recv()
    for j in range(1, 8):
        res_copy(j).wait_send()
    group = iota((8, 128), 1) // 16
    lower_rows = jnp.zeros((8, 128), F32)
    upper_rows = jnp.zeros((8, 128), F32)
    for i in range(8):
        lower_rows = jnp.where(group == i, rcv[i], lower_rows)
        upper_rows = jnp.where(group == (i + 4) % 8, rcv[i], upper_rows)
    out[0:8, :] = lower_rows
    out[8:12, :] = pltpu.roll(upper_rows, 64, 1)[0:4, :]


def shards(
    slabs,
    features,
    coords,
    send_rows,
    send_count,
    neighbours,
    neighbour_count,
    geom_weight,
    feat_weight,
    bias_one,
    hidden_weight,
    bias_two,
    out_weight,
    bias_three,
):
    points = features.shape[1]
    send = send_rows.shape[1]
    pairs = 16 * neighbours.shape[1]
    args = (
        features,
        coords,
        send_rows,
        send_count.reshape(2),
        neighbours,
        neighbour_count,
        geom_weight.T,
        feat_weight,
        bias_one.reshape(1, -1),
        hidden_weight,
        bias_two.reshape(1, -1),
        out_weight.T,
        bias_three.reshape(1, -1),
    )
    dma = pltpu.SemaphoreType.DMA
    held = [
        (pltpu.SMEM if i in (3, 5) else pltpu.VMEM)(a.shape, a.dtype) for i, a in enumerate(args)
    ]
    return pl.pallas_call(
        functools.partial(kernel, slabs),
        out_shape=jax.ShapeDtypeStruct((12, 128), F32),
        in_specs=[pl.BlockSpec(memory_space=pltpu.HBM)] * len(args),
        out_specs=pl.BlockSpec(memory_space=pltpu.VMEM),
        scratch_shapes=held
        + [
            pltpu.VMEM((8, ROWS, points * 3 // 4), BF16),
            pltpu.VMEM((8, ROWS, send * 3 // 4), BF16),
            pltpu.VMEM((2, ROWS, send * 3 // 4), BF16),
            pltpu.VMEM((ROWS, send * 3 // 4), BF16),
            pltpu.VMEM((2, ROWS, send // 4), BF16),
            pltpu.VMEM((ROWS, send // 4), BF16),
            pltpu.VMEM((9 * ROWS, points + send), BF16),
            pltpu.VMEM((points + send, pairs), BF16),
            pltpu.VMEM((9 * ROWS, pairs), F32),
            pltpu.VMEM((80, pairs), F32),
            pltpu.VMEM((ROWS, points), F32),
            pltpu.VMEM((ROWS, points * 3 // 4), F32),
            pltpu.VMEM((128, 128), F32),
            pltpu.VMEM((208, 128), F32),
            pltpu.VMEM((80, 9 * ROWS), BF16),
            pltpu.VMEM((128, 80), BF16),
            pltpu.VMEM((8, 8, 128), F32),
            pltpu.VMEM((8, 8, 128), F32),
            dma((len(args),)),
            dma((4,)),
            dma((8,)),
            dma((3,)),
            dma((2,)),
            dma((2,)),
            dma((8,)),
            dma((4,)),
            dma((1,)),
            dma((3,)),
            dma((2,)),
            dma((1,)),
            dma((7,)),
            dma((8,)),
        ],
        compiler_params=pltpu.CompilerParams(
            collective_id=0, has_side_effects=True, vmem_limit_bytes=48 * 2**20
        ),
    )(*[pltpu.with_memory_space_constraint(a, pltpu.HBM) for a in args])


def solution(mesh):
    placed = (
        P("chan", "slab"),
        P(None, "slab"),
        P(None, "slab"),
        P(None, "slab"),
        P("slab", None),
        P("slab"),
        P(),
        P(),
        P(),
        P(),
        P(),
        P(),
        P(),
    )
    return jax.shard_map(
        functools.partial(shards, mesh.shape["slab"]),
        mesh=mesh,
        in_specs=placed,
        out_specs=P("chan", "slab"),
        check_vma=False,
    )
```

```python
import functools

import jax
import jax.numpy as jnp
from jax import lax
from jax.experimental import pallas as pl
from jax.experimental.pallas import tpu as pltpu
from jax.sharding import PartitionSpec as P

MESH = pl.DeviceIdType.MESH
ZD = 2
GX = 16
GY = 4
F32 = jnp.float32
BF16 = jnp.bfloat16
ROWS = 16
BLK = 256
C0 = 0.7978845608028654
C1 = 0.7978845608028654 * 0.044715


def gelu(x):
    half = 0.5 * x
    return half + half * jnp.tanh(x * (C0 + C1 * (x * x)))


def iota(shape, dim):
    return lax.broadcasted_iota(jnp.int32, shape, dim)


def one_hot(index, ramp):
    row = jnp.broadcast_to(index, (16, index.shape[1])).astype(BF16)
    full = jnp.concatenate([row] * (BLK // 16), axis=0)
    return jnp.where(ramp == full, jnp.ones_like(full), jnp.zeros_like(full))


def kernel(
    slabs,
    feat_h,
    coords_h,
    send_rows_h,
    send_count_h,
    nbr_h,
    counts_h,
    geom_h,
    feat_weight_h,
    bias_one_h,
    hidden_weight_h,
    bias_two_h,
    out_weight_h,
    bias_three_h,
    out,
    feat,
    coords,
    send_rows,
    send_count,
    nbr,
    counts,
    geom_t,
    feat_weight,
    bias_one,
    hidden_weight,
    bias_two,
    out_t,
    bias_three,
    own,
    halo,
    picked,
    passing,
    side_out,
    side_in,
    table,
    hot,
    grid,
    node,
    stage,
    pack,
    small,
    wide,
    w_pre,
    w_out,
    res,
    rcv,
    in_sem,
    own_send,
    own_recv,
    own_fwd,
    halo_send,
    far_send,
    halo_recv,
    halo_fwd,
    pass_recv,
    z_send,
    side_send,
    side_recv,
    res_send,
    res_recv,
):
    s = lax.axis_index("slab")
    c = lax.axis_index("chan")
    chip = c // 2
    core = c % 2
    sib = c + 1 - 2 * core
    front = 1 - chip // 2
    ends = 1 - (chip + 1) // 2 % 2
    half = s * 2 // slabs
    begins = s == slabs // 2

    def works_upper(slab):
        usual = jnp.where(slab * 2 // slabs == 0, front, 1 - front)
        return jnp.where(slab == slabs // 2, ends, usual)

    upper = works_upper(s)
    rank = 2 * jnp.where(begins, jnp.where(ends == 1, chip // 3, chip - 1), chip % 2) + core
    place = 4 * upper + rank
    early = (half == 0) & (front == 1)
    has_up = s < slabs - 1
    has_down = s > 0
    has = (has_down, has_up)
    has_halo = jnp.where(upper == 1, s < slabs - 1, s > 0)
    distant = (s == slabs // 2, s == slabs // 2 - 1)
    near = tuple(has[d] & jnp.logical_not(distant[d]) for d in range(2))
    plane_far = jnp.where(upper == 1, s == slabs // 2 - 1, s == slabs // 2)
    plane_near = has_halo & jnp.logical_not(plane_far)
    beside = 2 * jnp.where(begins, 3 - chip, chip + 1 - 2 * (chip % 2)) + core

    points = feat.shape[1]
    send = send_rows.shape[1]
    body = points * 3 // 4
    tail = points - body
    hbody = send * 3 // 4
    htail = send - hbody
    pairs = node.shape[1]

    barrier = pltpu.get_barrier_semaphore()
    for j in range(1, 8):
        pl.semaphore_signal(barrier, inc=1, device_id=(s, (c + j) % 8), device_id_type=MESH)

    for d in range(2):

        @pl.when(near[d])
        def _():
            pl.semaphore_signal(
                barrier, inc=1, device_id=(s - 1 + 2 * d, c), device_id_type=MESH
            )

        @pl.when(distant[d] & (upper == d))
        def _():
            for q in range(4):
                pl.semaphore_signal(
                    barrier,
                    inc=1,
                    device_id=(s - 1 + 2 * d, 2 * q + core),
                    device_id_type=MESH,
                )

    loads = [
        pltpu.make_async_copy(a, b, in_sem.at[i])
        for i, (a, b) in enumerate(
            [
                (feat_h, feat),
                (coords_h, coords),
                (send_rows_h, send_rows),
                (send_count_h, send_count),
                (nbr_h, nbr),
                (counts_h, counts),
                (geom_h, geom_t),
                (feat_weight_h, feat_weight),
                (bias_one_h, bias_one),
                (hidden_weight_h, hidden_weight),
                (bias_two_h, bias_two),
                (out_weight_h, out_t),
                (bias_three_h, bias_three),
            ]
        )
    ]
    for load in loads:
        load.start()
    for load in loads[:6]:
        load.wait()

    values = feat[...].astype(F32)
    pack[0:12, :] = values[:, 0:body]
    for g in range(3):
        pack[12:16, g * tail : (g + 1) * tail] = values[4 * g : 4 * g + 4, body:points]
    own[c] = pack[...].astype(BF16)

    stage[0:12, :] = values
    stage[12:15, :] = coords[...].astype(F32)
    stage[15:16, :] = jnp.ones((1, points), F32)
    slot = stage[...].astype(BF16)

    ramp = iota((BLK, 128), 0).astype(F32).astype(BF16)
    pieces = points // BLK
    stacked = jnp.concatenate([slot[:, h * BLK : (h + 1) * BLK] for h in range(pieces)], axis=0)
    for d in range(2):
        idx = send_rows[d : d + 1, :]
        idx = jnp.where(iota((1, send), 1) < send_count[d], idx, -1)
        low = (idx & (BLK - 1)).astype(F32)
        high = lax.shift_right_arithmetic(idx, 8)
        hots = jnp.concatenate(
            [one_hot(low[:, t * 128 : (t + 1) * 128], ramp) for t in range(send // 128)], axis=1
        )
        parts = jnp.dot(stacked, hots, preferred_element_type=F32)
        total = jnp.zeros((ROWS, send), F32)
        for h in range(pieces):
            total = total + jnp.where(high == h, parts[h * ROWS : (h + 1) * ROWS], 0.0)
        pack[0:12, 0:hbody] = total[0:12, 0:hbody]
        for g in range(3):
            pack[12:16, g * htail : (g + 1) * htail] = total[4 * g : 4 * g + 4, hbody:send]
        picked[d] = pack[:, 0:hbody].astype(BF16)
        for j in range(4):
            pack[4 * j : 4 * j + 4, 0:htail] = total[12:16, j * htail : (j + 1) * htail]
        side_out[d] = pack[:, 0:htail].astype(BF16)

    first = pl.multiple_of(place * 16, 16)
    idx = nbr[pl.ds(first, 16), :]
    idx = idx - jnp.where(idx >= points, send * upper, 0)
    slots = iota((1, 128), 1)
    rows = []
    for n in range(16):
        rows.append(jnp.where(slots < counts[first + n], idx[n : n + 1, :], -1))
    lows = [(r & (BLK - 1)).astype(F32) for r in rows]
    highs = [lax.shift_right_arithmetic(r, 8) for r in rows]

    def build(kb, carry):
        at = pl.ds(pl.multiple_of(kb * BLK, BLK), BLK)
        for n in range(16):
            pick = jnp.where(highs[n] == kb, lows[n], -1.0)
            hot[at, n * 128 : (n + 1) * 128] = one_hot(pick, ramp)
        return carry

    steps = (points + send) // BLK

    @pl.when(early)
    def _():
        lax.fori_loop(0, steps, build, 0)

    others = [jnp.where(has[d], jnp.where(distant[d], 2, 1), 0) for d in range(2)]
    pl.semaphore_wait(barrier, 7 + others[0] + others[1])

    def remote(src, dst, sem_out, sem_in, target):
        return pltpu.make_async_remote_copy(
            src_ref=src,
            dst_ref=dst,
            send_sem=sem_out,
            recv_sem=sem_in,
            device_id=target,
            device_id_type=MESH,
        )

    def list_copy(d, direct):
        return remote(
            picked.at[d],
            halo.at[c] if direct else passing,
            halo_send.at[d],
            halo_recv.at[c] if direct else pass_recv.at[0],
            (s - 1 + 2 * d, c),
        )

    def far_copy(d, q):
        return remote(
            picked.at[d],
            halo.at[c],
            far_send.at[q],
            halo_recv.at[c],
            (s - 1 + 2 * d, 2 * (q + d) + core),
        )

    def side_copy(d, target):
        return remote(
            side_out.at[d], side_in, side_send.at[d], side_recv.at[0], (s - 1 + 2 * d, target)
        )

    def there_of(j):
        up = j - 1 + jnp.where(chip <= j - 1, 1, 0)
        down = 4 - j - jnp.where(3 - chip <= j - 1, 1, 0)
        return jnp.where(chip < 2, down, up)

    def own_copy(j):
        target = sib if j == 0 else 2 * there_of(j) + core
        return remote(own.at[c], own.at[c], own_send.at[j], own_recv.at[c], (s, target))

    def when_list(d, act):
        @pl.when(distant[d])
        def _():
            for q in range(2):
                act(far_copy(d, q))

            @pl.when((ends if d == 1 else 1 - front) == 1)
            def _():
                there = jnp.where(chip == 3, 1, 2) if d == 1 else 3 - chip
                act(side_copy(d, 2 * there + core))

        used = works_upper(s - 1 + 2 * d) == 1 - d

        @pl.when(near[d] & used)
        def _():
            act(list_copy(d, True))
            act(side_copy(d, c))

        @pl.when(near[d] & jnp.logical_not(used))
        def _():
            act(list_copy(d, False))

    for d in (1, 0):
        when_list(d, lambda copy: copy.start())
    for j in (1, 2, 3, 0):
        own_copy(j).start()

    def landed(buf, sem, i):
        return remote(buf.at[i], buf.at[i], sem.at[i], sem.at[i], (s, sib))

    def forward(buf, fwd, recv, i, k):
        return remote(buf.at[i], buf.at[i], fwd.at[k], recv.at[i], (s, sib))

    def same_plane():
        return remote(halo.at[c], halo.at[c], z_send.at[0], halo_recv.at[c], (s, beside))

    def other_plane(q):
        return remote(
            passing,
            halo.at[c],
            z_send.at[1 + q],
            halo_recv.at[c],
            (s, 2 * jnp.where(begins, jnp.where(ends == 1, 1 + q, 3 * q), 2 * front + q) + core),
        )

    def when_pass(d, act):
        @pl.when(near[d] & (upper == d))
        def _():
            act(same_plane())

        @pl.when(near[d] & (upper != d))
        def _():
            for q in range(2):
                act(other_plane(q))

    def pass_near():
        for d in range(2):

            @pl.when(near[d] & (upper != d))
            def _():
                remote(passing, passing, pass_recv.at[0], pass_recv.at[0], (s, sib)).wait_recv()
                for q in range(2):
                    other_plane(q).start()

        for d in range(2):

            @pl.when(near[d] & (upper == d))
            def _():
                landed(halo, halo_recv, c).wait_recv()
                same_plane().start()
                forward(halo, halo_fwd, halo_recv, c, 0).start()

    for load in loads[6:]:
        load.wait()
    small[...] = jnp.zeros_like(small)
    small[0:6, 0:80] = geom_t[...].astype(F32)
    small[6:7, 0:80] = bias_one[...]
    small[7:8, 0:80] = bias_two[...]
    lane = iota((96, 128), 1)
    spread = jnp.where(
        (lane // ROWS * 12 + lane % ROWS == iota((96, 128), 0)) & (lane % ROWS < 12), 1.0, 0.0
    )
    small[8:16, :] = jnp.dot(
        jnp.broadcast_to(bias_three[...], (8, 96)),
        spread,
        preferred_element_type=F32,
        precision=lax.Precision.HIGHEST,
    )
    cols = jnp.transpose(small[...])
    spread = spread.astype(BF16)
    w_pre[:, 0:128] = jnp.dot(feat_weight[...], spread, preferred_element_type=F32).astype(BF16)
    lane16 = iota((80, 16), 1)
    w_side = jnp.zeros((80, 16), F32)
    for i in range(3):
        w_side = jnp.where(lane16 == i, cols[0:80, 3 + i : 4 + i], w_side)
    w_pre[:, 128:144] = w_side.astype(BF16)
    small[0:80, :] = jnp.dot(out_t[...], spread, preferred_element_type=F32)
    w_out[...] = jnp.transpose(small[...])[:, 0:80].astype(BF16)
    along_y = ((rank % GY).astype(F32) + 0.5) / GY
    along_z = ((2 * s + upper).astype(F32) + 0.5) / (ZD * slabs)
    wide[0:80, :] = jnp.broadcast_to(cols[0:80, 7:8], (80, 128))
    wide[80:208, :] = jnp.broadcast_to(cols[:, 8:9], (128, 128))
    slope = jnp.broadcast_to(cols[0:80, 0:1], (80, 128))
    base = jnp.broadcast_to(
        cols[0:80, 1:2] * along_y + cols[0:80, 2:3] * along_z + cols[0:80, 6:7], (80, 128)
    )
    for n in range(16):
        node[:, n * 128 : (n + 1) * 128] = base + slope * ((n + 0.5) / GX)

    @pl.when(jnp.logical_not(early))
    def _():
        lax.fori_loop(0, steps // 2, build, 0)

    pass_near()

    @pl.when(jnp.logical_not(early))
    def _():
        lax.fori_loop(steps // 2, steps, build, 0)

    extra = jnp.concatenate(
        [coords[...].astype(F32), jnp.ones((1, points), F32), jnp.zeros((12, points), F32)], axis=0
    )
    table[128:144, 0:points] = extra.astype(BF16)

    for j in range(1, 4):
        i = 2 * ((chip + j) % 4) + core
        landed(own, own_recv, i).wait_recv()
        forward(own, own_fwd, own_recv, i, j - 1).start()

    for j in range(4):
        landed(own, own_recv, 2 * ((chip + j) % 4) + 1 - core).wait_recv()

    table[0:128, 0:body] = own[:, :, 0:body].reshape(128, body)
    for i in range(8):
        rest = own[i].astype(F32)[12:16, :]
        rest = jnp.concatenate(
            [rest[:, g * tail : (g + 1) * tail] for g in range(3)] + [jnp.zeros((4, tail), F32)], axis=0
        )
        table[i * ROWS : (i + 1) * ROWS, body:points] = rest.astype(BF16)
    cut = pairs * 4 // 8

    def gather_own(low, high):
        grid[:, low:high] = jnp.dot(
            table[:, 0:points], hot[0:points, low:high], preferred_element_type=F32
        )

    gather_own(0, cut)

    @pl.when(plane_near)
    def _():
        for q in range(1, 4):
            i = 2 * ((chip + q) % 4) + core
            landed(halo, halo_recv, i).wait_recv()
            forward(halo, halo_fwd, halo_recv, i, q).start()

    gather_own(cut, pairs)

    @pl.when(plane_far)
    def _():
        for q in range(4):
            i = 2 * (3 - q) + core
            landed(halo, halo_recv, i).wait_recv()
            forward(halo, halo_fwd, halo_recv, i, q).start()

    @pl.when(has_halo)
    def _():
        side_copy(0, c).wait_recv()
        for q in range(4):
            landed(halo, halo_recv, 2 * q + 1 - core).wait_recv()

    @pl.when(jnp.logical_not(has_halo))
    def _():
        halo[...] = jnp.zeros_like(halo)
        side_in[...] = jnp.zeros_like(side_in)

    table[0:128, points : points + hbody] = halo[...].reshape(128, hbody)
    for i in range(8):
        rest = halo[i].astype(F32)[12:16, :]
        rest = jnp.concatenate(
            [rest[:, g * htail : (g + 1) * htail] for g in range(3)] + [jnp.zeros((4, htail), F32)],
            axis=0,
        )
        table[i * ROWS : (i + 1) * ROWS, points + hbody : points + send] = rest.astype(BF16)
    rest = side_in[...].astype(F32)
    rest = jnp.concatenate([rest[4 * j : 4 * j + 4, :] for j in range(4)], axis=1)
    rest = jnp.concatenate([rest, jnp.zeros((12, send), F32)], axis=0)
    table[128:144, points : points + send] = rest.astype(BF16)

    values = grid[...] + jnp.dot(
        table[:, points : points + send],
        hot[points : points + send, :],
        preferred_element_type=F32,
    )
    pre = jnp.dot(w_pre[...], values.astype(BF16), preferred_element_type=F32)
    h1 = gelu(pre.astype(BF16).astype(F32) + node[...]).astype(BF16)
    h2 = jnp.dot(hidden_weight[...], h1, preferred_element_type=F32)
    h2 = gelu(h2 + jnp.concatenate([wide[0:80, :]] * 16, axis=1)).astype(BF16)
    kappa = jnp.dot(w_out[...], h2, preferred_element_type=F32)
    kappa = kappa + jnp.concatenate([wide[80:208, :]] * 16, axis=1)
    prod = kappa * values[0:128, :]

    lane8 = iota((8, 8, 128), 2)
    lane1 = iota((1, 128), 1)
    low_at = place * 16
    high_at = (place + 4) % 8 * 16
    acc = jnp.zeros((8, 8, 128), F32)
    number = jnp.ones((1, 128), F32)
    for n in range(16):
        at = slice(n * 128, (n + 1) * 128)
        total = jnp.sum(prod[:, at], axis=1, keepdims=True).reshape(8, ROWS, 1)
        acc = jnp.where(
            lane8 == low_at + n,
            total[:, 0:8],
            jnp.where(lane8 == high_at + n, total[:, 8:16], acc),
        )
        used = jnp.sum(values[128:136, at], axis=1, keepdims=True)[3:4]
        number = jnp.where((lane1 == low_at + n) | (lane1 == high_at + n), used, number)
    res[...] = acc / number[None]

    def res_copy(j):
        target = sib if j == 7 else 2 * there_of((j + 1) // 2) + (j - 1) % 2
        return remote(
            res.at[target], rcv.at[place], res_send.at[j - 1], res_recv.at[place], (s, target)
        )

    for j in range(1, 8):
        res_copy(j).start()
    rcv[place] = res[c]

    for j in range(4):
        own_copy(j).wait_send()
    for j in range(1, 4):
        forward(own, own_fwd, own_recv, c, j - 1).wait_send()
    for d in (1, 0):
        when_list(d, lambda copy: copy.wait_send())

    for d in range(2):
        when_pass(d, lambda copy: copy.wait_send())

    @pl.when(has_halo)
    def _():
        for q in range(4):
            forward(halo, halo_fwd, halo_recv, 2 * q + core, q).wait_send()

    for j in range(1, 8):
        landed(rcv, res_recv, (place + j) % 8).wait_recv()
    for j in range(1, 8):
        res_copy(j).wait_send()
    group = iota((8, 128), 1) // 16
    lower_rows = jnp.zeros((8, 128), F32)
    upper_rows = jnp.zeros((8, 128), F32)
    for i in range(8):
        lower_rows = jnp.where(group == i, rcv[i], lower_rows)
        upper_rows = jnp.where(group == (i + 4) % 8, rcv[i], upper_rows)
    out[0:8, :] = lower_rows
    out[8:12, :] = pltpu.roll(upper_rows, 64, 1)[0:4, :]


def finish(source, out):
    out[...] = source[...]


def shards(
    slabs,
    features,
    coords,
    send_rows,
    send_count,
    neighbours,
    neighbour_count,
    geom_weight,
    feat_weight,
    bias_one,
    hidden_weight,
    bias_two,
    out_weight,
    bias_three,
):
    points = features.shape[1]
    send = send_rows.shape[1]
    pairs = 16 * neighbours.shape[1]
    args = (
        features,
        coords,
        send_rows,
        send_count.reshape(2),
        neighbours,
        neighbour_count,
        geom_weight.T,
        feat_weight,
        bias_one.reshape(1, -1),
        hidden_weight,
        bias_two.reshape(1, -1),
        out_weight.T,
        bias_three.reshape(1, -1),
    )
    dma = pltpu.SemaphoreType.DMA
    held = [
        (pltpu.SMEM if i in (3, 5) else pltpu.VMEM)(a.shape, a.dtype) for i, a in enumerate(args)
    ]
    result = pl.pallas_call(
        functools.partial(kernel, slabs),
        out_shape=jax.ShapeDtypeStruct((12, 128), F32),
        in_specs=[pl.BlockSpec(memory_space=pltpu.HBM)] * len(args),
        out_specs=pl.BlockSpec(memory_space=pltpu.VMEM),
        scratch_shapes=held
        + [
            pltpu.VMEM((8, ROWS, points * 3 // 4), BF16),
            pltpu.VMEM((8, ROWS, send * 3 // 4), BF16),
            pltpu.VMEM((2, ROWS, send * 3 // 4), BF16),
            pltpu.VMEM((ROWS, send * 3 // 4), BF16),
            pltpu.VMEM((2, ROWS, send // 4), BF16),
            pltpu.VMEM((ROWS, send // 4), BF16),
            pltpu.VMEM((9 * ROWS, points + send), BF16),
            pltpu.VMEM((points + send, pairs), BF16),
            pltpu.VMEM((9 * ROWS, pairs), F32),
            pltpu.VMEM((80, pairs), F32),
            pltpu.VMEM((ROWS, points), F32),
            pltpu.VMEM((ROWS, points * 3 // 4), F32),
            pltpu.VMEM((128, 128), F32),
            pltpu.VMEM((208, 128), F32),
            pltpu.VMEM((80, 9 * ROWS), BF16),
            pltpu.VMEM((128, 80), BF16),
            pltpu.VMEM((8, 8, 128), F32),
            pltpu.VMEM((8, 8, 128), F32),
            dma((len(args),)),
            dma((4,)),
            dma((8,)),
            dma((3,)),
            dma((2,)),
            dma((2,)),
            dma((8,)),
            dma((4,)),
            dma((1,)),
            dma((3,)),
            dma((2,)),
            dma((1,)),
            dma((7,)),
            dma((8,)),
        ],
        compiler_params=pltpu.CompilerParams(
            collective_id=0, has_side_effects=True, vmem_limit_bytes=48 * 2**20
        ),
    )(*[pltpu.with_memory_space_constraint(a, pltpu.HBM) for a in args])
    return pl.pallas_call(
        finish,
        out_shape=jax.ShapeDtypeStruct((12, 128), F32),
        in_specs=[pl.BlockSpec(memory_space=pltpu.VMEM)],
        out_specs=pl.BlockSpec(memory_space=pltpu.VMEM),
        compiler_params=pltpu.CompilerParams(vmem_limit_bytes=2**20),
    )(result)


def solution(mesh):
    placed = (
        P("chan", "slab"),
        P(None, "slab"),
        P(None, "slab"),
        P(None, "slab"),
        P("slab", None),
        P("slab"),
        P(),
        P(),
        P(),
        P(),
        P(),
        P(),
        P(),
    )
    return jax.shard_map(
        functools.partial(shards, mesh.shape["slab"]),
        mesh=mesh,
        in_specs=placed,
        out_specs=P("chan", "slab"),
        check_vma=False,
    )
```
